512 devices in a mesh: samp: 4 (over z_lo), row: 16 (over y, x), col: 8 (over z_hi, core).
Axes of the slice: x: 4, y: 4, z: 16 (z_hi: 4, z_lo: 4; z = z_hi * 4 + z_lo), core: 2. Of those that a mesh axis runs over, the one named last changes fastest.
Arguments:
- genotypes: int32 [2048, 8192], P('samp', 'row'), may hold values from 0 to 2, as said below
- frequencies: float32 [8192], P('row'), may hold values from 0.25 to 0.5, as said below
- trait_scores: float32 [64, 8192], P(None, 'row'), may hold values from -6 to 6
- typed_mask: int32 [8192], P('row'), may hold values 0 or 1
- panel_index: int32 [1], replicated, may hold values from 0 to 511
Outputs:
- conditioned: float32 [8192, 8192], P('row', 'col')
- whitened: float32 [64, 1024], replicated
- residual: float32 [64, 8192], P(None, 'row')
The draws below stay inside these ranges and needn't reach their ends.
Inputs may be any that keep to these rules, and one draw needn't show every extreme that they name: `genotypes`: each sample's dosage at a variant is its number of the variant's allele over two haplotypes, with the allele's chance the variant's frequency. frequencies are multiples of 1/64.
All inputs are finite; a program needn't handle non-finite values. No bound on the sum of `typed_mask` on one device may be relied on, other than what follows from the above.
Results may differ from the reference program's by a relative error of at most 0.0045.
Values may be sent and summed in bfloat16 or wider, within the bound.
A program may use at most 64 MiB of HBM per device.

```python
import jax
import jax.numpy as jnp
from jax import lax

B = 1024
TRAITS = 64
V = 8192
SAMPLES = 2048
N_COL = 8


block_span = 32


def allele_levels(key):
    return jax.random.randint(jax.random.fold_in(key, 11), (V,), 16, 33)


def draw_frequencies(key, part):
    return allele_levels(key).astype(jnp.float32) / 64.0


def haplotype_alleles(key, levels, which):
    blocks = V // block_span
    shared = jax.random.randint(jax.random.fold_in(key, 20 + which), (SAMPLES, blocks), 0, 64)
    shared_full = jnp.repeat(shared, block_span, axis=1)
    own = jax.random.randint(jax.random.fold_in(key, 30 + which), (SAMPLES, V), 0, 64)
    mixing = jax.random.randint(jax.random.fold_in(key, 40 + which), (SAMPLES, V), 0, 10)
    draws = jnp.where(mixing < 9, shared_full, own)
    return (draws < levels[None, :]).astype(jnp.int32)


def draw_genotypes(key, part):
    levels = allele_levels(key)
    first = haplotype_alleles(key, levels, 0)
    second = haplotype_alleles(key, levels, 1)
    return (first + second).astype(jnp.int32)


def place_ends(entries, own_key, low, high):
    longest = entries.shape.index(max(entries.shape))
    spots = []
    for shift in (0, 1):
        where = [jax.random.randint(jax.random.fold_in(own_key, axis), (), 0, length) for axis, length in enumerate(entries.shape)]
        where[longest] = (where[longest] + shift) % entries.shape[longest]
        spots.append(tuple(where))
    return entries.at[spots[0]].set(low).at[spots[1]].set(high)


def level_of(stream_key, extent, shards, low, high):
    factor_of = 1.0
    for dim, shards_of in shards:
        steps = jax.random.uniform(jax.random.fold_in(jax.random.fold_in(stream_key, 6), dim), (shards_of,), jnp.float32, low / len(shards), high / len(shards))
        factor_of = factor_of * jnp.repeat(jnp.exp(steps), extent[dim] // shards_of).reshape((-1,) + (1,) * (len(extent) - 1 - dim))
    return factor_of


def bell_draw(rng, extent, deviation, reach, pieces=(), kind=jnp.bfloat16):
    result = deviation * jax.random.normal(rng, extent, jnp.float32)
    if pieces:
        result = result * level_of(rng, extent, pieces, -0.22, 0.18)
    return jnp.clip(result, -reach, reach).astype(kind)


def setup_inputs(seed: int = 0) -> dict:
    splits = jax.random.split(jax.random.key(seed), 6)
    genotypes = draw_genotypes(jax.random.fold_in(splits[5], 71), 0)
    frequencies = draw_frequencies(jax.random.fold_in(splits[5], 71), 0)
    trait_scores = bell_draw(splits[2], (TRAITS, V), 1.0, 6.0, ((1, 16),), jnp.float32)
    typed_mask = place_ends((jax.random.randint(splits[3], (V,), 0, 4) < 3).astype(jnp.int32), jax.random.fold_in(splits[3], 1), 0, 1)
    panel_index = jax.random.randint(splits[4], (1,), 0, 64 * N_COL).astype(jnp.int32)
    return dict(genotypes=genotypes, frequencies=frequencies, trait_scores=trait_scores, typed_mask=typed_mask, panel_index=panel_index)


ridge = 0.1

def reference(genotypes, frequencies, trait_scores, typed_mask, panel_index):
    spread = jnp.sqrt(2.0 * frequencies * (1.0 - frequencies))
    standard = ((genotypes.astype(jnp.float32) - 2.0 * frequencies) / spread).astype(jnp.bfloat16)
    values = standard.astype(jnp.float32)
    linkage = jnp.dot(values.T, values, precision=lax.Precision.HIGHEST) / SAMPLES
    linkage = linkage + ridge * jnp.eye(V, dtype=jnp.float32)
    start = (panel_index[0] % N_COL * B).astype(jnp.int32)
    panel_slab = lax.dynamic_slice_in_dim(linkage, start, B, 1)
    diag_block = lax.dynamic_slice_in_dim(panel_slab, start, B, 0)
    factor = jnp.linalg.cholesky(diag_block)
    panel_factor = lax.linalg.triangular_solve(factor, panel_slab, left_side=False, lower=True, transpose_a=True)
    conditioned = linkage - jnp.dot(panel_factor, panel_factor.T, precision=lax.Precision.HIGHEST)
    masked = trait_scores * typed_mask.astype(jnp.float32)
    masked_panel = lax.dynamic_slice_in_dim(masked, start, B, 1)
    whitened = lax.linalg.triangular_solve(factor, masked_panel, left_side=False, lower=True, transpose_a=True)
    residual = masked - jnp.dot(whitened, panel_factor.T, precision=lax.Precision.HIGHEST)
    return (conditioned, whitened, residual)
```

```python
import functools

import jax
import jax.numpy as jnp
from jax import lax
from jax.experimental import pallas as pl
from jax.experimental.pallas import tpu as pltpu
from jax.sharding import PartitionSpec as P

ridge = 0.1
NT = (((1,), (1,)), ((), ()))
TN = (((0,), (0,)), ((), ()))
f32, bf16 = jnp.float32, jnp.bfloat16


def split2(x):
    h = x.astype(bf16)
    return h, (x - h.astype(f32)).astype(bf16)


def split3(x):
    h = x.astype(bf16)
    r = x - h.astype(f32)
    m = r.astype(bf16)
    return h, m, (r - m.astype(f32)).astype(bf16)


def pivots(x_ref, t):
    j0 = pl.multiple_of(t * 16, 16)
    block = x_ref[pl.ds(j0, 16), :128]
    block = pltpu.roll(block, lax.rem(128 - j0, 128), 1)
    a = {}
    for i in range(16):
        for k in range(i + 1):
            a[i, k] = jnp.broadcast_to(block[i : i + 1, k : k + 1], (1, 128))
    rows = [x_ref[pl.ds(j0 + i, 1), :] for i in range(16)]
    for k in range(16):
        r = lax.rsqrt(a[k, k])
        rec = r * r
        m = {}
        if k < 15:
            sq = a[k + 1, k] * a[k + 1, k]
        for i in range(k + 1, 16):
            m[i] = a[i, k] * rec
        for i in range(k + 1, 16):
            for j in range(k + 1, i + 1):
                if i == j == k + 1:
                    a[i, j] = a[i, j] - sq * rec
                else:
                    a[i, j] = a[i, j] - m[i] * a[j, k]
        for i in range(k + 1, 16):
            rows[i] = rows[i] - jnp.concatenate([m[i], m[i]], axis=1) * rows[k]
        x_ref[pl.ds(j0 + k, 1), :] = rows[k] * jnp.concatenate([r, r], axis=1)
    u = x_ref[pl.ds(j0, 16), :]
    h, m, l = split3(u)
    rhs = jnp.concatenate([h, m, h, l, h, m], axis=0)
    left = jnp.concatenate([h, h, m, h, l, m], axis=0)[:, :128].astype(f32)
    lane = lax.broadcasted_iota(jnp.int32, left.shape, 1)
    left = jnp.where(lane >= j0 + 16, left, 0.0).astype(bf16)
    x_ref[...] = x_ref[...] - lax.dot_general(left, rhs, TN, preferred_element_type=f32)


def k2(panel, rows_at, cols_at, n, s_ref, mask_p_ref, mask_r_ref, cond_ref, whit_ref, res_ref,
       x_ref, w_ref, hi_ref, lo_ref):
    groups, total, depth = s_ref.shape
    traits = mask_p_ref.shape[0]
    nr, nc = cond_ref.shape
    samples = groups * depth
    blocks = n // 128
    eye = (lax.broadcasted_iota(jnp.int32, (128, 128), 0) == lax.broadcasted_iota(jnp.int32, (128, 128), 1)).astype(f32)

    def start_of(chunk):
        if chunk < blocks:
            return panel * n + chunk * 128
        if chunk < blocks + nr // 128:
            return rows_at + (chunk - blocks) * 128
        return cols_at + (chunk - blocks - nr // 128) * 128

    def covered(at, rows, b):
        k = b * 128
        ah, al = hi_ref[pl.ds(at, rows), :k], lo_ref[pl.ds(at, rows), :k]
        fh, fl = hi_ref[pl.ds(b * 128, 128), :k], lo_ref[pl.ds(b * 128, 128), :k]
        dot = functools.partial(lax.dot_general, dimension_numbers=NT, preferred_element_type=f32)
        return dot(ah, fh) + dot(ah, fl) + dot(al, fh)

    def chunk_value(chunk, b):
        at = chunk * 128
        acc = jnp.zeros((128, 128), f32)
        for g in range(groups):
            acc = acc + lax.dot_general(s_ref[g, pl.ds(at, 128), :], s_ref[g, pl.ds(b * 128, 128), :], NT, preferred_element_type=f32)
        acc = acc / samples
        here = (start_of(chunk) == panel * n + b * 128).astype(f32)
        acc = acc + eye * (ridge * here)
        if b:
            acc = acc - covered(at, 128, b)
        return acc

    for b in range(blocks):
        x_ref[:, :128] = chunk_value(b, b)
        x_ref[:, 128:] = eye

        def body(t, _):
            pivots(x_ref, t)
            return 0

        lax.fori_loop(0, 8, body, 0)
        inv_h, inv_l = split2(x_ref[:, 128:])
        inv = jnp.concatenate([inv_h, inv_l, inv_h], axis=1)
        for chunk in range(b + 1, total // 128):
            w_ref[pl.ds(chunk * 128, 128), :] = chunk_value(chunk, b)
        tr = mask_p_ref[:, b * 128 : (b + 1) * 128]
        if b:
            tr = tr - covered(total, traits, b)
        w_ref[pl.ds(total, traits), :] = tr

        def finish(at, rows):
            wh, wl = split2(w_ref[pl.ds(at, rows), :])
            out = lax.dot_general(jnp.concatenate([wh, wh, wl], axis=1), inv, NT, preferred_element_type=f32)
            h, l = split2(out)
            hi_ref[pl.ds(at, rows), b * 128 : (b + 1) * 128] = h
            lo_ref[pl.ds(at, rows), b * 128 : (b + 1) * 128] = l
            return out

        for chunk in range(b + 1, total // 128):
            finish(chunk * 128, 128)
        whit_ref[:, b * 128 : (b + 1) * 128] = finish(total, traits)

    dot = functools.partial(lax.dot_general, dimension_numbers=NT, preferred_element_type=f32)
    r0, c0 = n, n + nr
    for i in range(nr // 128):
        for j in range(nc // 256):
            acc = jnp.zeros((128, 256), f32)
            for g in range(groups):
                acc = acc + dot(s_ref[g, pl.ds(r0 + i * 128, 128), :], s_ref[g, pl.ds(c0 + j * 256, 256), :])
            acc = acc / samples
            ids = lax.broadcasted_iota(jnp.int32, (128, 256), 0) + (rows_at + i * 128)
            jds = lax.broadcasted_iota(jnp.int32, (128, 256), 1) + (cols_at + j * 256)
            acc = acc + jnp.where(ids == jds, ridge, 0.0)
            ah, al = hi_ref[pl.ds(r0 + i * 128, 128), :], lo_ref[pl.ds(r0 + i * 128, 128), :]
            bh, bl = hi_ref[pl.ds(c0 + j * 256, 256), :], lo_ref[pl.ds(c0 + j * 256, 256), :]
            cond_ref[i * 128 : (i + 1) * 128, j * 256 : (j + 1) * 256] = acc - (dot(ah, bh) + dot(ah, bl) + dot(al, bh))
    th, tl = hi_ref[pl.ds(total, traits), :], lo_ref[pl.ds(total, traits), :]
    rh, rl = hi_ref[pl.ds(r0, nr), :], lo_ref[pl.ds(r0, nr), :]
    res_ref[...] = mask_r_ref[...] - (dot(th, rh) + dot(th, rl) + dot(tl, rh))


def call_k2(where, s, mask_p, mask_r, n=1024, nr=512, nc=1024, **kw):
    traits = mask_p.shape[0]
    total = s.shape[1]

    def kernel(where_ref, *refs):
        k2(where_ref[0], where_ref[1], where_ref[2], n, *refs)

    vmem = pl.BlockSpec(memory_space=pltpu.VMEM)
    return pl.pallas_call(
        kernel,
        out_shape=(
            jax.ShapeDtypeStruct((nr, nc), f32),
            jax.ShapeDtypeStruct((traits, n), f32),
            jax.ShapeDtypeStruct((traits, nr), f32),
        ),
        in_specs=[pl.BlockSpec(memory_space=pltpu.SMEM), vmem, vmem, vmem],
        out_specs=(vmem, vmem, vmem),
        scratch_shapes=[
            pltpu.VMEM((128, 256), f32),
            pltpu.VMEM((total + traits, 128), f32),
            pltpu.VMEM((total + traits, n), bf16),
            pltpu.VMEM((total + traits, n), bf16),
        ],
        compiler_params=pltpu.CompilerParams(vmem_limit_bytes=50 * 1024 * 1024),
        **kw,
    )(where, s, mask_p, mask_r)


MESH = pl.DeviceIdType.MESH


def gather(g_ref, f_ref, tr_ref, tm_ref, panel_ref, s_ref, mp_ref, mk_ref, own_ref, yb, pp, xb, ym, pm, xm, yc, sems):
    (y1s, y1r, x1s, x1r, z1s, z1r, d1s, d1r, z0s, z0r, d0s, d0r, y2s, y2r, x2s, x2r, yms, ymr, xms, xmr, dms, dmr) = sems
    s = lax.axis_index("samp")
    r = lax.axis_index("row")
    c = lax.axis_index("col")
    y, x = r // 4, lax.rem(r, 4)
    zh, core = c // 2, lax.rem(c, 2)
    q = lax.rem(panel_ref[0], 8)
    n, nr = 1024, 512

    def at(dy=0, dx=0, dz=0, core_to=None):
        ny = lax.rem(y + dy + 4, 4)
        nx = lax.rem(x + dx + 4, 4)
        nz = lax.rem(zh * 4 + s + dz + 16, 16)
        k = core if core_to is None else core_to
        return (lax.rem(nz, 4), ny * 4 + nx, nz // 4 * 2 + k)

    sibling = at(core_to=1 - core)

    def remote(src, dst, send, recv, to):
        copy = pltpu.make_async_remote_copy(src_ref=src, dst_ref=dst, send_sem=send, recv_sem=recv, device_id=to, device_id_type=MESH)
        copy.start()
        return copy

    barrier = pltpu.get_barrier_semaphore()
    partners = [at(dy=d) for d in (1, 2, 3)]
    partners += [at(dx=d, core_to=k) for d in (1, 2, 3) for k in (0, 1)]
    partners += [at(dz=d) for d in (-2, -1, 1, 2)] + [sibling]
    for to in partners:
        pl.semaphore_signal(barrier, inc=1, device_id=to, device_id_type=MESH)

    freq = f_ref[...]
    spread = jnp.sqrt(2.0 * freq * (1.0 - freq))
    for k in range(4):
        lanes = slice(k * 128, (k + 1) * 128)
        value = (g_ref[:, lanes].astype(f32) - 2.0 * freq[:, lanes]) / spread[:, lanes]
        own_ref[lanes, :] = value.T.astype(bf16)
    mk_ref[...] = tr_ref[...] * tm_ref[...].astype(f32)
    half = pl.multiple_of(core * 256, 256)
    s_ref[s, pl.ds(n + half, 256), :] = own_ref[pl.ds(half, 256), :]
    pl.semaphore_wait(barrier, len(partners))

    sent = []
    for k in range(4):
        mine = own_ref.at[pl.ds(pl.multiple_of(k * 128 + core * 64, 64), 64)]
        for d in (1, 2, 3):
            sent.append(remote(mine, yb[k].at[d - 1], y1s.at[k, d - 1], y1r.at[k, d - 1], at(dy=-d)))
    for i, (dz, start, size) in enumerate(((1, 0, 256), (-1, 0, 256), (2, 0, 128), (-2, 128, 128))):
        sent.append(remote(own_ref.at[pl.ds(pl.multiple_of(half + start, 128), size)],
                           s_ref.at[s, pl.ds(pl.multiple_of(n + half + start, 128), size)], z0s.at[i], z0r.at[i], at(dz=dz)))
    mrow = pl.multiple_of(core * 32, 32)
    for d in (1, 2, 3):
        sent.append(remote(mk_ref.at[pl.ds(mrow, 32)], ym.at[d - 1], yms.at[d - 1], ymr.at[d - 1], at(dy=-d)))

    def landed(ref, sem):
        pltpu.make_async_copy(ref, ref, sem).wait()

    def pick(distance, mine, others):
        out = mine
        for d in (1, 2, 3):
            out = jnp.where(distance == d, others[d - 1], out)
        return out

    dy = lax.rem(q // 2 - y + 4, 4)
    for k in range(4):
        for d in (1, 2, 3):
            landed(yb[k].at[d - 1], y1r.at[k, d - 1])
        mine = own_ref[pl.ds(pl.multiple_of(k * 128 + core * 64, 64), 64), :]
        pp[k, :, :] = pick(dy, mine, [yb[k][d - 1] for d in (1, 2, 3)])
        for d in (1, 2, 3):
            sent.append(remote(pp.at[k], xb[k].at[d - 1], x1s.at[k, d - 1], x1r.at[k, d - 1], at(dx=-d)))
    for d in (1, 2, 3):
        landed(ym.at[d - 1], ymr.at[d - 1])
    pm[...] = pick(dy, mk_ref[pl.ds(mrow, 32), :], [ym[d - 1] for d in (1, 2, 3)])
    for d in (1, 2, 3):
        sent.append(remote(pm, xm.at[d - 1], xms.at[d - 1], xmr.at[d - 1], at(dx=-d)))

    for k in range(4):
        for d in (1, 2, 3):
            landed(xb[k].at[d - 1], x1r.at[k, d - 1])
        for h in range(2):
            dx = lax.rem(lax.rem(q, 2) * 2 + h - x + 4, 4)
            base = h * 512 + k * 128 + core * 64
            to = pl.ds(pl.multiple_of(base, 64), 64)
            s_ref[s, to, :] = pick(dx, pp[k], [xb[k][d - 1] for d in (1, 2, 3)])
            for i, (dz, start, size) in enumerate(((1, 0, 64), (-1, 0, 64), (2, 0, 32), (-2, 32, 32))):
                part = s_ref.at[s, pl.ds(pl.multiple_of(base + start, 32), size)]
                sent.append(remote(part, part, z1s.at[k, h, i], z1r.at[k, h, i], at(dz=dz)))

    def hear(base, half_size, recv):
        for i, (dz, start, size) in enumerate(((1, 0, 2 * half_size), (-1, 0, 2 * half_size), (2, 0, half_size), (-2, half_size, half_size))):
            group = lax.rem(s - dz + 4, 4)
            landed(s_ref.at[group, pl.ds(pl.multiple_of(base + start, 32), size)], recv(i))

    across = []
    for k in range(4):
        for h in range(2):
            base = h * 512 + k * 128 + core * 64
            hear(base, 32, lambda i: z1r.at[k, h, i])
            part = s_ref.at[:, pl.ds(pl.multiple_of(base, 64), 64)]
            across.append(remote(part, part, d1s.at[k, h], d1r.at[k, h], sibling))

    hear(n + half, 128, lambda i: z0r.at[i])
    mine = s_ref.at[:, pl.ds(pl.multiple_of(n + half, 256), 256)]
    across.append(remote(mine, mine, d0s.at[0], d0r.at[0], sibling))

    @pl.when(y == zh)
    def _():
        pltpu.make_async_copy(mine, yc, y2r.at[0]).start()
        for d in (1, 2, 3):
            remote(mine, yc, y2s.at[d - 1], y2r.at[0], at(dy=d))

    for d in (1, 2, 3):
        landed(xm.at[d - 1], xmr.at[d - 1])
    for h in range(2):
        dx = lax.rem(lax.rem(q, 2) * 2 + h - x + 4, 4)
        mp_ref[pl.ds(mrow, 32), h * 512 : (h + 1) * 512] = pick(dx, pm[...], [xm[d - 1] for d in (1, 2, 3)])
    part = mp_ref.at[pl.ds(mrow, 32)]
    across.append(remote(part, part, dms.at[0], dmr.at[0], sibling))

    landed(yc, y2r.at[0])
    slot = lax.rem(x, 2) * 2 + core
    place = s_ref.at[:, pl.ds(pl.multiple_of(n + nr + slot * 256, 256), 256)]
    for d in (1, 2, 3):
        sent.append(remote(yc, place, x2s.at[d - 1], x2r.at[slot], at(dx=d, core_to=x // 2)))

    @pl.when(core == x // 2)
    def _():
        pltpu.make_async_copy(yc, place, x2r.at[slot]).start()

    @pl.when(core != x // 2)
    def _():
        remote(yc, place, x2s.at[3], x2r.at[slot], sibling)

    for i in range(4):
        landed(s_ref.at[:, pl.ds(n + nr + i * 256, 256)], x2r.at[i])
    for copy in across:
        copy.wait()
    for copy in sent:
        copy.wait_send()

    @pl.when(y == zh)
    def _():
        for d in (1, 2, 3):
            landed(yc, y2s.at[d - 1])

    @pl.when(core != x // 2)
    def _():
        landed(yc, x2s.at[3])


def call_gather(genotypes, frequencies, scores, typed, panel_index):
    vmem = pl.BlockSpec(memory_space=pltpu.VMEM)
    dma = pltpu.SemaphoreType.DMA
    n_sems = 22

    def kernel(g, f, tr, tm, panel, s, mp, mk, own, *rest):
        yb, rest = rest[:4], rest[4:]
        pp, rest = rest[0], rest[1:]
        xb, rest = rest[:4], rest[4:]
        ym, pm, xm, yc = rest[:4]
        gather(g, f, tr, tm, panel, s, mp, mk, own, yb, pp, xb, ym, pm, xm, yc, rest[4:])

    return pl.pallas_call(
        kernel,
        out_shape=(
            jax.ShapeDtypeStruct((4, 2560, 512), bf16),
            jax.ShapeDtypeStruct((64, 1024), f32),
            jax.ShapeDtypeStruct((64, 512), f32),
        ),
        in_specs=[vmem] * 4 + [pl.BlockSpec(memory_space=pltpu.SMEM)],
        out_specs=(vmem,) * 3,
        scratch_shapes=[
            pltpu.VMEM((512, 512), bf16),
            *[pltpu.VMEM((3, 64, 512), bf16)] * 4,
            pltpu.VMEM((4, 64, 512), bf16),
            *[pltpu.VMEM((3, 64, 512), bf16)] * 4,
            pltpu.VMEM((3, 32, 512), f32),
            pltpu.VMEM((32, 512), f32),
            pltpu.VMEM((3, 32, 512), f32),
            pltpu.VMEM((4, 256, 512), bf16),
            dma((4, 3)), dma((4, 3)), dma((4, 3)), dma((4, 3)),
            dma((4, 2, 4)), dma((4, 2, 4)), dma((4, 2)), dma((4, 2)),
            dma((4,)), dma((4,)), dma((1,)), dma((1,)),
            dma((3,)), dma((1,)), dma((4,)), dma((4,)),
            dma((3,)), dma((3,)), dma((3,)), dma((3,)), dma((1,)), dma((1,)),
        ],
        compiler_params=pltpu.CompilerParams(vmem_limit_bytes=40 * 1024 * 1024, collective_id=0, has_side_effects=True),
    )(genotypes, frequencies, scores, typed, panel_index)


def on_device(genotypes, frequencies, trait_scores, typed_mask, panel_index):
    s, masked_panel, masked = call_gather(genotypes, frequencies[None, :], trait_scores, typed_mask[None, :], panel_index)
    where = jnp.stack([panel_index[0] % 8, lax.axis_index("row") * 512, lax.axis_index("col") * 1024]).astype(jnp.int32)
    return call_k2(where, s, masked_panel, masked)


def solution(mesh):
    placed = (P("samp", "row"), P("row"), P(None, "row"), P("row"), P())
    return jax.shard_map(
        on_device,
        mesh=mesh,
        in_specs=placed,
        out_specs=(P("row", "col"), P(), P(None, "row")),
        check_vma=False,
    )
```

```python
import functools

import jax
import jax.numpy as jnp
from jax import lax
from jax.experimental import pallas as pl
from jax.experimental.pallas import tpu as pltpu
from jax.sharding import PartitionSpec as P

MESH = pl.DeviceIdType.MESH

ridge = 0.1
NT = (((1,), (1,)), ((), ()))
TN = (((0,), (0,)), ((), ()))
f32, bf16 = jnp.float32, jnp.bfloat16
n, nr, nc, traits, samples = 1024, 512, 1024, 64, 2048
R0, C0 = n, n + nr
T0 = n + nr
I0 = T0 + traits


def split2(x):
    h = x.astype(bf16)
    return h, (x - h.astype(f32)).astype(bf16)


def split3(x):
    h = x.astype(bf16)
    r = x - h.astype(f32)
    m = r.astype(bf16)
    return h, m, (r - m.astype(f32)).astype(bf16)


dot = functools.partial(lax.dot_general, dimension_numbers=NT, preferred_element_type=f32)


def spread(x, i, k):
    return jnp.broadcast_to(x[i : i + 1, k : k + 1], (8, 128))


def twice(x):
    return jnp.concatenate([x, x], axis=1)


def eight(x_ref, at, a, rows, below):
    cols, pairs, extra = below
    for k in range(8):
        r = lax.rsqrt(a[k, k])
        rec = r * r
        if k < 7:
            square = a[k + 1, k] * a[k + 1, k]
        m = {i: a[i, k] * rec for i in range(k + 1, 8)}
        for i in range(k + 1, 8):
            for j in range(k + 1, i + 1):
                if i == j == k + 1:
                    a[i, j] = a[i, j] - square * rec
                else:
                    a[i, j] = a[i, j] - m[i] * a[j, k]
        for i in range(k + 1, 8):
            rows[i] = rows[i] - twice(m[i]) * rows[k]
            if extra:
                extra[i] = extra[i] - m[i] * extra[k]
        if cols:
            m2 = cols[k] * rec
            for j in range(k + 1, 8):
                cols[j] = cols[j] - m2 * a[j, k]
            pairs[0] = pairs[0] - twice(m2) * rows[k]
            pairs[1] = pairs[1] - m2 * extra[k]
        x_ref[pl.ds(at + k, 1), :] = (rows[k] * twice(r))[:1]


def pivots(x_ref, t):
    j0 = pl.multiple_of(t * 16, 16)
    block = pltpu.roll(x_ref[pl.ds(j0, 16), :128], lax.rem(128 - j0, 128), 1)
    top, low = block[:8], block[8:]
    rows = [jnp.broadcast_to(x_ref[pl.ds(j0 + i, 1), :], (8, 256)) for i in range(8)]
    a = {(i, k): spread(top, i, k) for i in range(8) for k in range(i + 1)}
    cols = [jnp.broadcast_to(low[:, k : k + 1], (8, 128)) for k in range(8)]
    extra = [jnp.broadcast_to(top[i : i + 1], (8, 128)) for i in range(8)]
    pairs = [x_ref[pl.ds(j0 + 8, 8), :], low]
    eight(x_ref, j0, a, rows, (cols, pairs, extra))
    rows = [jnp.broadcast_to(pairs[0][i : i + 1], (8, 256)) for i in range(8)]
    a = {(i, k): spread(pairs[1], i, 8 + k) for i in range(8) for k in range(i + 1)}
    eight(x_ref, j0 + 8, a, rows, (None, None, None))


def update(x_ref, t):
    j0 = pl.multiple_of(t * 16, 16)
    u = x_ref[pl.ds(j0, 16), :]
    h, m, l = split3(u)
    rhs = jnp.concatenate([h, m, h, l, h, m], axis=0)
    left = jnp.concatenate([h, h, m, h, l, m], axis=0)[:, :128].astype(f32)
    lane = lax.broadcasted_iota(jnp.int32, left.shape, 1)
    left = jnp.where(lane >= j0 + 16, left, 0.0).astype(bf16)
    x_ref[...] = x_ref[...] - lax.dot_general(left, rhs, TN, preferred_element_type=f32)


def joined(ref, rows, lanes):
    h, l = ref[0][rows, lanes], ref[1][rows, lanes]
    return jnp.concatenate([h, h, l], axis=1), jnp.concatenate([h, l, h], axis=1)


def eliminate(panel, rows_at, cols_at, s_ref, mask_p_ref, mask_r_ref, cond_ref, whit_ref, res_ref,
              x_ref, w_ref, hi_ref, lo_ref, g_ref, h_ref, service=lambda b, part: None):
    both = (hi_ref, lo_ref)
    iota = functools.partial(lax.broadcasted_iota, jnp.int32)
    eye = (iota((128, 128), 0) == iota((128, 128), 1)).astype(f32)

    def block(b):
        return slice(b * 128, (b + 1) * 128)

    def start(b):
        w = w_ref.at[b % 2]
        w[b * 128 : R0, :] = jnp.zeros((R0 - b * 128, 128), f32)
        w[block(b), :] = eye * ridge
        ids = iota((nr, 128), 0) + (rows_at - panel * n - b * 128)
        w[R0:T0, :] = jnp.where(ids == iota((nr, 128), 1), ridge, 0.0)
        w[T0:I0, :] = mask_p_ref[:, block(b)]
        if b:
            w[I0 : I0 + b * 128, :] = jnp.zeros((b * 128, 128), f32)
        w[I0 + b * 128 : I0 + (b + 1) * 128, :] = eye

    hi_ref[...] = jnp.zeros_like(hi_ref)
    lo_ref[...] = jnp.zeros_like(lo_ref)
    g_ref[...] = jnp.zeros_like(g_ref)
    start(0)
    acc = dot(s_ref[0, :T0, :], s_ref[0, :128, :])
    for g in range(1, 4):
        acc = acc + dot(s_ref[g, :T0, :], s_ref[g, :128, :])
    w_ref[0, :T0, :] = w_ref[0, :T0, :] + acc * (1.0 / samples)

    for b in range(8):
        service(b, 0)
        now, later = w_ref.at[b % 2], w_ref.at[(b + 1) % 2]
        x_ref[:, :128] = now[block(b), :]
        x_ref[:, 128:] = eye
        low, high = (b + 1) * 128, I0 + (b + 1) * 128
        rows = slice(low, high)
        if b < 7:
            start(b + 1)

        def body(t, earlier):
            pivots(x_ref, t)
            if b < 7:
                lanes = pl.ds(pl.multiple_of(lax.rem(t, 2) * 256, 256), 256)
                new = dot(s_ref[t // 2, low:T0, lanes], s_ref[t // 2, low : low + 128, lanes]) * (1.0 / samples)
                if earlier:
                    lanes = pl.ds(pl.multiple_of(t * 128, 128), 128)
                    taken = dot(joined(both, rows, lanes)[0], joined(both, slice(low, low + 128), lanes)[1])
                    later[low:T0, :] = later[low:T0, :] + (new - taken[: T0 - low])
                    later[T0:high, :] = later[T0:high, :] - taken[T0 - low :]
                else:
                    later[low:T0, :] = later[low:T0, :] + new
            if earlier:
                lanes = block(b - 1)
                to = pl.ds(pl.multiple_of(t * 128, 128), 128)
                right = joined(both, pl.ds(pl.multiple_of(I0 + t * 128, 64), 128), lanes)[1]
                g_ref[:, to] = g_ref[:, to] + dot(joined(both, slice(R0, T0), lanes)[0], right)
            update(x_ref, t)

        if b:
            pl.loop(0, b)(functools.partial(body, earlier=True))
        service(b, 1)
        pl.loop(b, 8)(functools.partial(body, earlier=False))
        inv_h, inv_l = split2(x_ref[:, 128:])
        wh, wl = split2(now[rows, :])
        out = dot(jnp.concatenate([wh, wh, wl], axis=1), jnp.concatenate([inv_h, inv_l, inv_h], axis=1))
        h, l = split2(out)
        hi_ref[rows, block(b)] = h
        lo_ref[rows, block(b)] = l
        whit_ref[:, block(b)] = out[T0 - low : I0 - low]
        if b < 7:
            later[rows, :] = later[rows, :] - dot(jnp.concatenate([h, h, l], axis=1), jnp.concatenate([h, l, h], axis=1)[:128])

    left = joined(both, slice(R0, T0), block(7))[0]
    g_ref[...] = g_ref[...] + dot(left, joined(both, slice(I0, I0 + n), block(7))[1])

    @pl.loop(0, 4)
    def _(g):
        gh, gl = split2(g_ref[...])
        taken = jnp.dot(gh, s_ref[g, :n, :], preferred_element_type=f32) + jnp.dot(gl, s_ref[g, :n, :], preferred_element_type=f32)
        h_ref[g] = (s_ref[g, R0:C0, :].astype(f32) - taken).astype(bf16)

    service(8, 0)
    same = jnp.where(cols_at == panel * n, ridge, 0.0)

    @pl.loop(0, 4)
    def _(j):
        at = pl.multiple_of(j * 256, 256)
        acc = dot(h_ref[0], s_ref[0, pl.ds(C0 + at, 256), :])
        for g in range(1, 4):
            acc = acc + dot(h_ref[g], s_ref[g, pl.ds(C0 + at, 256), :])
        ids = iota((nr, 256), 0) + (rows_at - cols_at - at)
        acc = acc * (1.0 / samples) + jnp.where(ids == iota((nr, 256), 1), ridge, 0.0)
        cond_ref[:, pl.ds(at, 256)] = acc - same * g_ref[:, pl.ds(at, 256)]

    th, tl = hi_ref[T0:I0, :], lo_ref[T0:I0, :]
    rh, rl = hi_ref[R0:T0, :], lo_ref[R0:T0, :]
    res_ref[...] = mask_r_ref[...] - (dot(th, rh) + dot(th, rl) + dot(tl, rh))


def eliminate_scratch():
    return [
        pltpu.VMEM((128, 256), f32),
        pltpu.VMEM((2, I0 + n, 128), f32),
        pltpu.VMEM((I0 + n, n), bf16),
        pltpu.VMEM((I0 + n, n), bf16),
        pltpu.VMEM((nr, n), f32),
        pltpu.VMEM((4, nr, samples // 4), bf16),
    ]


def gather(ins, panel_ref, g_ref, f_ref, tr_ref, tm_ref, s_ref, mp_ref, mk_ref, own_ref, yb, pp, xb, ym, pm, xm, yc, sems):
    ins_sem, sems = sems[0], sems[1:]
    (y1s, y1r, x1s, x1r, z1s, z1r, d1s, d1r, z0s, z0r, d0s, d0r, y2s, y2r, x2s, x2r, x3s, yms, ymr, xms, xmr, dms, dmr) = sems
    s = lax.axis_index("samp")
    r = lax.axis_index("row")
    c = lax.axis_index("col")
    y, x = r // 4, lax.rem(r, 4)
    zh, core = c // 2, lax.rem(c, 2)
    q = lax.rem(panel_ref[0], 8)

    def at(dy=0, dx=0, dz=0, core_to=None):
        ny = lax.rem(y + dy + 4, 4)
        nx = lax.rem(x + dx + 4, 4)
        nz = lax.rem(zh * 4 + s + dz + 16, 16)
        k = core if core_to is None else core_to
        return (lax.rem(nz, 4), ny * 4 + nx, nz // 4 * 2 + k)

    loads = [pltpu.make_async_copy(src, dst, ins_sem.at[i]) for i, (src, dst) in enumerate(zip(ins, (g_ref, f_ref, tr_ref, tm_ref)))]
    for load in loads:
        load.start()
    sibling = at(core_to=1 - core)

    def remote(src, dst, send, recv, to):
        copy = pltpu.make_async_remote_copy(src_ref=src, dst_ref=dst, send_sem=send, recv_sem=recv, device_id=to, device_id_type=MESH)
        copy.start()
        return copy

    barrier = pltpu.get_barrier_semaphore()
    partners = [at(dy=d) for d in (1, 2, 3)]
    partners += [at(dx=d, core_to=k) for d in (1, 2, 3) for k in (0, 1)]
    partners += [at(dz=d) for d in (-2, -1, 1, 2)] + [sibling]
    for to in partners:
        pl.semaphore_signal(barrier, inc=1, device_id=to, device_id_type=MESH)

    for load in loads:
        load.wait()
    freq = f_ref[...]
    spread = jnp.sqrt(2.0 * freq * (1.0 - freq))
    for k in range(4):
        lanes = slice(k * 128, (k + 1) * 128)
        value = (g_ref[:, lanes].astype(f32) - 2.0 * freq[:, lanes]) / spread[:, lanes]
        own_ref[lanes, :] = value.T.astype(bf16)
    mk_ref[...] = tr_ref[...] * tm_ref[...].astype(f32)
    half = pl.multiple_of(core * 256, 256)
    s_ref[s, pl.ds(n + half, 256), :] = own_ref[pl.ds(half, 256), :]
    pl.semaphore_wait(barrier, len(partners))

    sent = []
    for k in range(4):
        mine = own_ref.at[pl.ds(pl.multiple_of(k * 128 + core * 64, 64), 64)]
        for d in (1, 2, 3):
            sent.append(remote(mine, yb[k].at[d - 1], y1s.at[k, d - 1], y1r.at[k, d - 1], at(dy=-d)))
    for i, (dz, start, size) in enumerate(((1, 0, 256), (-1, 0, 256), (2, 0, 128), (-2, 128, 128))):
        sent.append(remote(own_ref.at[pl.ds(pl.multiple_of(half + start, 128), size)],
                           s_ref.at[s, pl.ds(pl.multiple_of(n + half + start, 128), size)], z0s.at[i], z0r.at[i], at(dz=dz)))
    mrow = pl.multiple_of(core * 32, 32)
    for d in (1, 2, 3):
        sent.append(remote(mk_ref.at[pl.ds(mrow, 32)], ym.at[d - 1], yms.at[d - 1], ymr.at[d - 1], at(dy=-d)))

    def landed(ref, sem):
        pltpu.make_async_copy(ref, ref, sem).wait()

    def pick(distance, mine, others):
        out = mine
        for d in (1, 2, 3):
            out = jnp.where(distance == d, others[d - 1], out)
        return out

    dy = lax.rem(q // 2 - y + 4, 4)
    for k in range(4):
        for d in (1, 2, 3):
            landed(yb[k].at[d - 1], y1r.at[k, d - 1])
        mine = own_ref[pl.ds(pl.multiple_of(k * 128 + core * 64, 64), 64), :]
        pp[k, :, :] = pick(dy, mine, [yb[k][d - 1] for d in (1, 2, 3)])
        for d in (1, 2, 3):
            sent.append(remote(pp.at[k], xb[k].at[d - 1], x1s.at[k, d - 1], x1r.at[k, d - 1], at(dx=-d)))
    for d in (1, 2, 3):
        landed(ym.at[d - 1], ymr.at[d - 1])
    pm[...] = pick(dy, mk_ref[pl.ds(mrow, 32), :], [ym[d - 1] for d in (1, 2, 3)])
    for d in (1, 2, 3):
        sent.append(remote(pm, xm.at[d - 1], xms.at[d - 1], xmr.at[d - 1], at(dx=-d)))

    for k in range(4):
        for d in (1, 2, 3):
            landed(xb[k].at[d - 1], x1r.at[k, d - 1])
        for h in range(2):
            dx = lax.rem(lax.rem(q, 2) * 2 + h - x + 4, 4)
            base = h * 512 + k * 128 + core * 64
            to = pl.ds(pl.multiple_of(base, 64), 64)
            s_ref[s, to, :] = pick(dx, pp[k], [xb[k][d - 1] for d in (1, 2, 3)])
            for i, (dz, start, size) in enumerate(((1, 0, 64), (-1, 0, 64), (2, 0, 32), (-2, 32, 32))):
                part = s_ref.at[s, pl.ds(pl.multiple_of(base + start, 32), size)]
                sent.append(remote(part, part, z1s.at[k, h, i], z1r.at[k, h, i], at(dz=dz)))

    def hear(base, half_size, recv):
        for i, (dz, start, size) in enumerate(((1, 0, 2 * half_size), (-1, 0, 2 * half_size), (2, 0, half_size), (-2, half_size, half_size))):
            group = lax.rem(s - dz + 4, 4)
            landed(s_ref.at[group, pl.ds(pl.multiple_of(base + start, 32), size)], recv(i))

    across = []
    for k in range(4):
        for h in range(2):
            base = h * 512 + k * 128 + core * 64
            hear(base, 32, lambda i: z1r.at[k, h, i])
            part = s_ref.at[:, pl.ds(pl.multiple_of(base, 64), 64)]
            across.append(remote(part, part, d1s.at[k, h], d1r.at[k, h], sibling))

    hear(n + half, 128, lambda i: z0r.at[i])
    mine = s_ref.at[:, pl.ds(pl.multiple_of(n + half, 256), 256)]
    across.append(remote(mine, mine, d0s.at[0], d0r.at[0], sibling))

    dist = lax.rem(y - zh + 4, 4)
    halves = [yc.at[2 * i : 2 * i + 2] for i in range(2)]

    def to_y(i, src, dy):
        pltpu.make_async_remote_copy(src_ref=src, dst_ref=halves[i], send_sem=y2s.at[i, (dy + 1) // 2], recv_sem=y2r.at[i],
                                     device_id=at(dy=dy), device_id_type=MESH).start()

    @pl.when(dist == 0)
    def _():
        parts = [s_ref.at[2 * i : 2 * i + 2, pl.ds(pl.multiple_of(n + half, 256), 256)] for i in range(2)]
        for i, dy in ((0, 1), (1, -1), (1, 1), (0, -1)):
            to_y(i, parts[i], dy)
        for i in range(2):
            pltpu.make_async_copy(parts[i], halves[i], y2r.at[i]).start()

    for d in (1, 2, 3):
        landed(xm.at[d - 1], xmr.at[d - 1])
    for h in range(2):
        dx = lax.rem(lax.rem(q, 2) * 2 + h - x + 4, 4)
        mp_ref[pl.ds(mrow, 32), h * 512 : (h + 1) * 512] = pick(dx, pm[...], [xm[d - 1] for d in (1, 2, 3)])
    part = mp_ref.at[pl.ds(mrow, 32)]
    across.append(remote(part, part, dms.at[0], dmr.at[0], sibling))


    target = x // 2
    slot = lax.rem(x, 2) * 2 + core

    def place(i, which):
        return s_ref.at[2 * i : 2 * i + 2, pl.ds(pl.multiple_of(n + nr + which * 256, 256), 256)]

    def to_x(i, src, which, sem, dx, k):
        pltpu.make_async_remote_copy(src_ref=src, dst_ref=place(i, which), send_sem=sem, recv_sem=x2r.at[which, i],
                                     device_id=at(dx=dx, core_to=k), device_id_type=MESH).start()

    def spread_half(i):
        landed(halves[i], y2r.at[i])

        @pl.when(dist == (1 if i == 0 else 3))
        def _():
            to_y(i, halves[i], 1 if i == 0 else -1)

        for dx in (1, -1):
            to_x(i, halves[i], slot, x2s.at[i, (dx + 1) // 2], dx, target)

        @pl.when(core == target)
        def _():
            pltpu.make_async_copy(halves[i], place(i, slot), x2r.at[slot, i]).start()

        @pl.when(core != target)
        def _():
            to_x(i, halves[i], slot, x2s.at[i, 2], 0, 1 - core)

    def relayed(i, e):
        return lax.rem(x - (core * 2 + e) + 4, 4) == (1 if i == 0 else 3)

    def relay(i):
        for e in range(2):

            @pl.when(relayed(i, e))
            def _():
                for c2 in range(2):
                    which = e * 2 + c2
                    landed(place(i, which), x2r.at[which, i])
                    to_x(i, place(i, which), which, x3s.at[which, i], 1 if i == 0 else -1, core)

    def arrive():
        for i in range(2):
            for e in range(2):

                @pl.when(jnp.logical_not(relayed(i, e)))
                def _():
                    for c2 in range(2):
                        landed(place(i, e * 2 + c2), x2r.at[e * 2 + c2, i])

    def drain():
        for copy in sent:
            copy.wait_send()
        for copy in across:
            copy.wait_send()
        for i in range(2):

            @pl.when(dist == 0)
            def _():
                for j in range(2):
                    landed(halves[i], y2s.at[i, j])

            @pl.when(dist == (1 if i == 0 else 3))
            def _():
                landed(halves[i], y2s.at[i, 1 if i == 0 else 0])

            for j in range(2):
                landed(halves[i], x2s.at[i, j])

            @pl.when(core != target)
            def _():
                landed(halves[i], x2s.at[i, 2])

            for e in range(2):

                @pl.when(relayed(i, e))
                def _():
                    for c2 in range(2):
                        landed(place(i, e * 2 + c2), x3s.at[e * 2 + c2, i])

    for copy in across:
        copy.wait_recv()
    return spread_half, relay, arrive, drain


def on_device(genotypes, frequencies, trait_scores, typed_mask, panel_index):
    dma = pltpu.SemaphoreType.DMA
    hbm, vmem = pl.BlockSpec(memory_space=pl.ANY), pl.BlockSpec(memory_space=pltpu.VMEM)
    own = eliminate_scratch()
    gathered = [
        pltpu.VMEM((512, 512), jnp.int32),
        pltpu.VMEM((1, 512), f32),
        pltpu.VMEM((traits, 512), f32),
        pltpu.VMEM((1, 512), jnp.int32),
        pltpu.VMEM((4, C0 + nc, 512), bf16),
        pltpu.VMEM((traits, n), f32),
        pltpu.VMEM((traits, 512), f32),
        pltpu.VMEM((512, 512), bf16),
        *[pltpu.VMEM((3, 64, 512), bf16)] * 4,
        pltpu.VMEM((4, 64, 512), bf16),
        *[pltpu.VMEM((3, 64, 512), bf16)] * 4,
        pltpu.VMEM((3, 32, 512), f32),
        pltpu.VMEM((32, 512), f32),
        pltpu.VMEM((3, 32, 512), f32),
        pltpu.VMEM((4, 256, 512), bf16),
    ]
    sems = [dma(shape) for shape in (
        (4,), (4, 3), (4, 3), (4, 3), (4, 3), (4, 2, 4), (4, 2, 4), (4, 2), (4, 2), (4,), (4,), (1,), (1,),
        (2, 2), (2,), (2, 3), (4, 2), (4, 2), (3,), (3,), (3,), (3,), (1,), (1,))]

    def kernel(g, f, tr, tm, panel_ref, cond_ref, whit_ref, res_ref, *rest):
        work, rest = rest[: len(own)], rest[len(own) :]
        bufs, rest = rest[: len(gathered)], rest[len(gathered) :]
        s_ref, mp_ref, mk_ref = bufs[4], bufs[5], bufs[6]
        yb, xb = bufs[8:12], bufs[13:17]
        spread_half, relay, arrive, drain = gather((g, f, tr, tm), panel_ref, *bufs[:8], yb, bufs[12], xb, *bufs[17:], rest)
        steps = {(0, 0): lambda: spread_half(0), (1, 0): lambda: spread_half(1), (3, 0): lambda: relay(0),
                 (5, 0): lambda: relay(1), (8, 0): arrive}

        def service(b, part):
            steps.get((b, part), lambda: None)()

        eliminate(lax.rem(panel_ref[0], 8), lax.axis_index("row") * 512, lax.axis_index("col") * 1024,
                  s_ref, mp_ref, mk_ref, cond_ref, whit_ref, res_ref, *work, service=service)
        drain()

    return pl.pallas_call(
        kernel,
        out_shape=(
            jax.ShapeDtypeStruct((nr, nc), f32),
            jax.ShapeDtypeStruct((traits, n), f32),
            jax.ShapeDtypeStruct((traits, nr), f32),
        ),
        in_specs=[hbm] * 4 + [pl.BlockSpec(memory_space=pltpu.SMEM)],
        out_specs=(vmem,) * 3,
        scratch_shapes=own + gathered + sems,
        compiler_params=pltpu.CompilerParams(vmem_limit_bytes=56 * 1024 * 1024, collective_id=0, has_side_effects=True),
    )(genotypes, frequencies[None, :], trait_scores, typed_mask[None, :], panel_index)


def solution(mesh):
    placed = (P("samp", "row"), P("row"), P(None, "row"), P("row"), P())
    return jax.shard_map(
        on_device,
        mesh=mesh,
        in_specs=placed,
        out_specs=(P("row", "col"), P(), P(None, "row")),
        check_vma=False,
    )
```

```python
import functools

import jax
import jax.numpy as jnp
from jax import lax
from jax.experimental import pallas as pl
from jax.experimental.pallas import tpu as pltpu
from jax.sharding import PartitionSpec as P

MESH = pl.DeviceIdType.MESH

ridge = 0.1
NT = (((1,), (1,)), ((), ()))
TN = (((0,), (0,)), ((), ()))
f32, bf16 = jnp.float32, jnp.bfloat16
n, nr, nc, traits, samples = 1024, 512, 1024, 64, 2048
R0, C0 = n, n + nr
T0 = n + nr
I0 = T0 + traits


def split2(x):
    h = x.astype(bf16)
    return h, (x - h.astype(f32)).astype(bf16)


def split3(x):
    h = x.astype(bf16)
    r = x - h.astype(f32)
    m = r.astype(bf16)
    return h, m, (r - m.astype(f32)).astype(bf16)


dot = functools.partial(lax.dot_general, dimension_numbers=NT, preferred_element_type=f32)


def spread(x, i, k):
    return jnp.broadcast_to(x[i : i + 1, k : k + 1], (8, 128))


def twice(x):
    return jnp.concatenate([x, x], axis=1)


def eight(x_ref, at, a, rows, below):
    cols, pairs, extra = below
    for k in range(8):
        r = lax.rsqrt(a[k, k])
        rec = r * r
        if k < 7:
            square = a[k + 1, k] * a[k + 1, k]
        m = {i: a[i, k] * rec for i in range(k + 1, 8)}
        for i in range(k + 1, 8):
            for j in range(k + 1, i + 1):
                if i == j == k + 1:
                    a[i, j] = a[i, j] - square * rec
                else:
                    a[i, j] = a[i, j] - m[i] * a[j, k]
        for i in range(k + 1, 8):
            rows[i] = rows[i] - twice(m[i]) * rows[k]
            if extra:
                extra[i] = extra[i] - m[i] * extra[k]
        if cols:
            m2 = cols[k] * rec
            for j in range(k + 1, 8):
                cols[j] = cols[j] - m2 * a[j, k]
            pairs[0] = pairs[0] - twice(m2) * rows[k]
            pairs[1] = pairs[1] - m2 * extra[k]
        x_ref[pl.ds(at + k, 1), :] = (rows[k] * twice(r))[:1]


def pivots(x_ref, t):
    j0 = pl.multiple_of(t * 16, 16)
    block = pltpu.roll(x_ref[pl.ds(j0, 16), :128], lax.rem(128 - j0, 128), 1)
    top, low = block[:8], block[8:]
    rows = [jnp.broadcast_to(x_ref[pl.ds(j0 + i, 1), :], (8, 256)) for i in range(8)]
    a = {(i, k): spread(top, i, k) for i in range(8) for k in range(i + 1)}
    cols = [jnp.broadcast_to(low[:, k : k + 1], (8, 128)) for k in range(8)]
    extra = [jnp.broadcast_to(top[i : i + 1], (8, 128)) for i in range(8)]
    pairs = [x_ref[pl.ds(j0 + 8, 8), :], low]
    eight(x_ref, j0, a, rows, (cols, pairs, extra))
    rows = [jnp.broadcast_to(pairs[0][i : i + 1], (8, 256)) for i in range(8)]
    a = {(i, k): spread(pairs[1], i, 8 + k) for i in range(8) for k in range(i + 1)}
    eight(x_ref, j0 + 8, a, rows, (None, None, None))


def update(x_ref, t):
    j0 = pl.multiple_of(t * 16, 16)
    u = x_ref[pl.ds(j0, 16), :]
    h, m, l = split3(u)
    rhs = jnp.concatenate([h, m, h, l, h, m], axis=0)
    left = jnp.concatenate([h, h, m, h, l, m], axis=0)[:, :128].astype(f32)
    lane = lax.broadcasted_iota(jnp.int32, left.shape, 1)
    left = jnp.where(lane >= j0 + 16, left, 0.0).astype(bf16)
    x_ref[...] = x_ref[...] - lax.dot_general(left, rhs, TN, preferred_element_type=f32)


def joined(ref, rows, lanes):
    h, l = ref[0][rows, lanes], ref[1][rows, lanes]
    return jnp.concatenate([h, h, l], axis=1), jnp.concatenate([h, l, h], axis=1)


def eliminate(panel, rows_at, cols_at, s_ref, mask_p_ref, mask_r_ref, cond_ref, whit_ref, res_ref,
              x_ref, w_ref, hi_ref, lo_ref, g_ref, h_ref, service=lambda b, part: None):
    both = (hi_ref, lo_ref)
    iota = functools.partial(lax.broadcasted_iota, jnp.int32)
    eye = (iota((128, 128), 0) == iota((128, 128), 1)).astype(f32)

    def block(b):
        return slice(b * 128, (b + 1) * 128)

    def start(b):
        w = w_ref.at[b % 2]
        w[b * 128 : R0, :] = jnp.zeros((R0 - b * 128, 128), f32)
        w[block(b), :] = eye * ridge
        ids = iota((nr, 128), 0) + (rows_at - panel * n - b * 128)
        w[R0:T0, :] = jnp.where(ids == iota((nr, 128), 1), ridge, 0.0)
        w[T0:I0, :] = mask_p_ref[:, block(b)]
        if b:
            w[I0 : I0 + b * 128, :] = jnp.zeros((b * 128, 128), f32)
        w[I0 + b * 128 : I0 + (b + 1) * 128, :] = eye

    start(0)
    acc = dot(s_ref[0, :T0, :], s_ref[0, :128, :])
    for g in range(1, 4):
        acc = acc + dot(s_ref[g, :T0, :], s_ref[g, :128, :])
    w_ref[0, :T0, :] = w_ref[0, :T0, :] + acc * (1.0 / samples)

    for b in range(8):
        service(b, 0)
        now, later = w_ref.at[b % 2], w_ref.at[(b + 1) % 2]
        x_ref[:, :128] = now[block(b), :]
        x_ref[:, 128:] = eye
        low, high = (b + 1) * 128, I0 + (b + 1) * 128
        rows = slice(low, high)
        if b < 7:
            start(b + 1)

        def body(t, earlier):
            pivots(x_ref, t)
            if b < 7:
                lanes = pl.ds(pl.multiple_of(lax.rem(t, 2) * 256, 256), 256)
                new = dot(s_ref[t // 2, low:T0, lanes], s_ref[t // 2, low : low + 128, lanes]) * (1.0 / samples)
                if earlier:
                    lanes = pl.ds(pl.multiple_of(t * 128, 128), 128)
                    taken = dot(joined(both, rows, lanes)[0], joined(both, slice(low, low + 128), lanes)[1])
                    later[low:T0, :] = later[low:T0, :] + (new - taken[: T0 - low])
                    later[T0:high, :] = later[T0:high, :] - taken[T0 - low :]
                else:
                    later[low:T0, :] = later[low:T0, :] + new
            if earlier:
                lanes = block(b - 1)
                to = pl.ds(pl.multiple_of(t * 128, 128), 128)
                right = joined(both, pl.ds(pl.multiple_of(I0 + t * 128, 64), 128), lanes)[1]
                g_ref[:, to] = g_ref[:, to] + dot(joined(both, slice(R0, T0), lanes)[0], right)
            update(x_ref, t)

        if b:
            pl.loop(0, b)(functools.partial(body, earlier=True))
        service(b, 1)
        pl.loop(b, 8)(functools.partial(body, earlier=False))
        inv_h, inv_l = split2(x_ref[:, 128:])
        wh, wl = split2(now[rows, :])
        out = dot(jnp.concatenate([wh, wh, wl], axis=1), jnp.concatenate([inv_h, inv_l, inv_h], axis=1))
        h, l = split2(out)
        hi_ref[rows, block(b)] = h
        lo_ref[rows, block(b)] = l
        whit_ref[:, block(b)] = out[T0 - low : I0 - low]
        if b < 7:
            later[rows, :] = later[rows, :] - dot(jnp.concatenate([h, h, l], axis=1), jnp.concatenate([h, l, h], axis=1)[:128])

    left = joined(both, slice(R0, T0), block(7))[0]
    g_ref[...] = g_ref[...] + dot(left, joined(both, slice(I0, I0 + n), block(7))[1])

    @pl.loop(0, 4)
    def _(g):
        gh, gl = split2(g_ref[...])
        taken = jnp.dot(gh, s_ref[g, :n, :], preferred_element_type=f32) + jnp.dot(gl, s_ref[g, :n, :], preferred_element_type=f32)
        h_ref[g] = (s_ref[g, R0:C0, :].astype(f32) - taken).astype(bf16)

    service(8, 0)
    same = jnp.where(cols_at == panel * n, ridge, 0.0)

    @pl.loop(0, 4)
    def _(j):
        at = pl.multiple_of(j * 256, 256)
        acc = dot(h_ref[0], s_ref[0, pl.ds(C0 + at, 256), :])
        for g in range(1, 4):
            acc = acc + dot(h_ref[g], s_ref[g, pl.ds(C0 + at, 256), :])
        ids = iota((nr, 256), 0) + (rows_at - cols_at - at)
        acc = acc * (1.0 / samples) + jnp.where(ids == iota((nr, 256), 1), ridge, 0.0)
        cond_ref[:, pl.ds(at, 256)] = acc - same * g_ref[:, pl.ds(at, 256)]

    th, tl = hi_ref[T0:I0, :], lo_ref[T0:I0, :]
    rh, rl = hi_ref[R0:T0, :], lo_ref[R0:T0, :]
    res_ref[...] = mask_r_ref[...] - (dot(th, rh) + dot(th, rl) + dot(tl, rh))


def eliminate_scratch():
    return [
        pltpu.VMEM((128, 256), f32),
        pltpu.VMEM((2, I0 + n, 128), f32),
        pltpu.VMEM((I0 + n, n), bf16),
        pltpu.VMEM((I0 + n, n), bf16),
        pltpu.VMEM((nr, n), f32),
        pltpu.VMEM((4, nr, samples // 4), bf16),
    ]


def gather(ins, panel_ref, g_ref, f_ref, tr_ref, tm_ref, s_ref, mp_ref, mk_ref, own_ref, yb, pp, xb, ym, pm, xm, yc, sems, meanwhile):
    (ins_sem, y1s, y1r, x1s, x1r, z1s, z1r, d1s, d1r, z0s, z0r, d0s, d0r, y2s, y2r, x2s, x2r, x3s, yms, ymr, xms, xmr, dms, dmr) = sems
    s = lax.axis_index("samp")
    r = lax.axis_index("row")
    c = lax.axis_index("col")
    y, x = r // 4, lax.rem(r, 4)
    zh, core = c // 2, lax.rem(c, 2)
    q = lax.rem(panel_ref[0], 8)

    def at(dy=0, dx=0, dz=0, core_to=None):
        ny = lax.rem(y + dy + 4, 4)
        nx = lax.rem(x + dx + 4, 4)
        nz = lax.rem(zh * 4 + s + dz + 16, 16)
        k = core if core_to is None else core_to
        return (lax.rem(nz, 4), ny * 4 + nx, nz // 4 * 2 + k)

    loads = [pltpu.make_async_copy(src, dst, ins_sem.at[i]) for i, (src, dst) in enumerate(zip(ins, (g_ref, f_ref, tr_ref, tm_ref)))]
    for load in loads:
        load.start()
    sibling = at(core_to=1 - core)
    sent, across = [], []

    def remote(src, dst, send, recv, to, kept=sent):
        copy = pltpu.make_async_remote_copy(src_ref=src, dst_ref=dst, send_sem=send, recv_sem=recv, device_id=to, device_id_type=MESH)
        copy.start()
        kept.append(copy)

    def landed(ref, sem):
        pltpu.make_async_copy(ref, ref, sem).wait()

    barrier = pltpu.get_barrier_semaphore()
    partners = [at(dy=d) for d in (-1, 1)]
    partners += [at(dx=d, core_to=k) for d in (-1, 1) for k in (0, 1)]
    partners += [at(dz=d) for d in (-1, 1)] + [sibling]
    for to in partners:
        pl.semaphore_signal(barrier, inc=1, device_id=to, device_id_type=MESH)
    for load in loads:
        load.wait()
    freq = f_ref[...]
    spread = jnp.sqrt(2.0 * freq * (1.0 - freq))
    for k in range(4):
        lanes = slice(k * 128, (k + 1) * 128)
        value = (g_ref[:, lanes].astype(f32) - 2.0 * freq[:, lanes]) / spread[:, lanes]
        own_ref[lanes, :] = value.T.astype(bf16)
    pl.semaphore_wait(barrier, len(partners))

    half = pl.multiple_of(core * 256, 256)
    mrow = pl.multiple_of(core * 32, 32)
    def send(src, slots, ss, rs, ways):
        for i in range(2):
            remote(src, slots.at[i], ss.at[i], rs.at[i], ways[i])

    def pass_on(slots, size, ss, rs, ways):
        for i in range(2):
            landed(slots.at[i], rs.at[i])
            part = pl.ds(i * size, size)
            remote(slots.at[i, part], slots.at[2, part], ss.at[2 + i], rs.at[2 + i], ways[i])

    def opposite(slots, size, rs):
        for i in range(2):
            landed(slots.at[2, pl.ds(i * size, size)], rs.at[2 + i])

    def pick(distance, mine, slots):
        out = jnp.where(distance == 1, slots[1], mine)
        out = jnp.where(distance == 3, slots[0], out)
        return jnp.where(distance == 2, slots[2], out)

    along_y, along_x = (at(dy=1), at(dy=-1)), (at(dx=1), at(dx=-1))
    along_z = (at(dz=1), at(dz=-1))
    for k in range(4):
        send(own_ref.at[pl.ds(pl.multiple_of(k * 128 + core * 64, 64), 64)], yb[k], y1s.at[k], y1r.at[k], along_y)

    def send_z(src, base, size, ss, rs):
        for i in range(2):
            remote(src, s_ref.at[s, pl.ds(base, size)], ss.at[i], rs.at[i], along_z[i])

    def pass_on_z(base, size, ss, rs):
        for i in range(2):
            group = lax.rem(s + (3 if i == 0 else 1), 4)
            landed(s_ref.at[group, pl.ds(base, size)], rs.at[i])
            part = s_ref.at[group, pl.ds(pl.multiple_of(base + i * size // 2, 32), size // 2)]
            remote(part, part, ss.at[2 + i], rs.at[2 + i], along_z[i])

    def opposite_z(base, size, rs):
        for i in range(2):
            landed(s_ref.at[lax.rem(s + 2, 4), pl.ds(pl.multiple_of(base + i * size // 2, 32), size // 2)], rs.at[2 + i])

    row_base = pl.multiple_of(n + half, 256)
    send_z(own_ref.at[pl.ds(half, 256)], row_base, 256, z0s, z0r)
    s_ref[s, pl.ds(row_base, 256), :] = own_ref[pl.ds(half, 256), :]
    mk_ref[...] = tr_ref[...] * tm_ref[...].astype(f32)
    send(mk_ref.at[pl.ds(mrow, 32)], ym, yms, ymr, along_y)
    meanwhile()

    for k in range(4):
        pass_on(yb[k], 32, y1s.at[k], y1r.at[k], along_y)
    pass_on_z(row_base, 256, z0s, z0r)
    dy = lax.rem(q // 2 - y + 4, 4)
    for k in range(4):
        opposite(yb[k], 32, y1r.at[k])
        mine = own_ref[pl.ds(pl.multiple_of(k * 128 + core * 64, 64), 64), :]
        pp[k, :, :] = pick(dy, mine, [yb[k][i] for i in range(3)])
        send(pp.at[k], xb[k], x1s.at[k], x1r.at[k], along_x)
    for k in range(4):
        pass_on(xb[k], 32, x1s.at[k], x1r.at[k], along_x)

    def panel_base(k, h):
        return pl.multiple_of(h * 512 + k * 128 + core * 64, 64)

    for k in range(4):
        opposite(xb[k], 32, x1r.at[k])
        for h in range(2):
            dx = lax.rem(lax.rem(q, 2) * 2 + h - x + 4, 4)
            base = panel_base(k, h)
            s_ref[s, pl.ds(base, 64), :] = pick(dx, pp[k], [xb[k][i] for i in range(3)])
            send_z(s_ref.at[s, pl.ds(base, 64)], base, 64, z1s.at[k, h], z1r.at[k, h])

    opposite_z(row_base, 256, z0r)
    mine = s_ref.at[:, pl.ds(row_base, 256)]
    remote(mine, mine, d0s.at[0], d0r.at[0], sibling, across)

    dist = lax.rem(y - zh + 4, 4)
    target = x // 2
    slot = lax.rem(x, 2) * 2 + core

    def half_of(i):
        return yc.at[pl.ds(2 * i, 2)]

    def to_y(i, src, sem, dy):
        pltpu.make_async_remote_copy(src_ref=src, dst_ref=half_of(i), send_sem=sem, recv_sem=y2r.at[i], device_id=at(dy=dy),
                                     device_id_type=MESH).start()

    @pl.when(dist == 0)
    def _():
        parts = [s_ref.at[2 * i : 2 * i + 2, pl.ds(row_base, 256)] for i in range(2)]
        for i, dy in ((0, 1), (1, -1), (1, 1), (0, -1)):
            to_y(i, parts[i], y2s.at[i, (dy + 1) // 2], dy)
        for i in range(2):
            pltpu.make_async_copy(parts[i], half_of(i), y2r.at[i]).start()

    pass_on(ym, 16, yms, ymr, along_y)
    opposite(ym, 16, ymr)
    pm[...] = pick(dy, mk_ref[pl.ds(mrow, 32), :], [ym[i] for i in range(3)])
    send(pm, xm, xms, xmr, along_x)

    def place(i, which):
        return s_ref.at[pl.ds(2 * i, 2), pl.ds(pl.multiple_of(n + nr + which * 256, 256), 256)]

    def to_x(i, src, which, sem, dx, k):
        pltpu.make_async_remote_copy(src_ref=src, dst_ref=place(i, which), send_sem=sem, recv_sem=x2r.at[which, i],
                                     device_id=at(dx=dx, core_to=k), device_id_type=MESH).start()

    def order(step):
        return jnp.where(dist == 3, 1 - step, step)

    def spread_half(step):
        i = order(step)
        landed(half_of(i), y2r.at[i])
        if step == 0:

            @pl.when(dist == 1)
            def _():
                to_y(0, half_of(0), y2s.at[0, 1], 1)

            @pl.when(dist == 3)
            def _():
                to_y(1, half_of(1), y2s.at[1, 0], -1)

        for dx in (1, -1):
            to_x(i, half_of(i), slot, x2s.at[i, (dx + 1) // 2], dx, target)

        @pl.when(core == target)
        def _():
            pltpu.make_async_copy(half_of(i), place(i, slot), x2r.at[slot, i]).start()

        @pl.when(core != target)
        def _():
            to_x(i, half_of(i), slot, x2s.at[i, 2], 0, 1 - core)

    def spread_near(step):
        @pl.when(dist != 2)
        def _():
            spread_half(step)

    def spread_far():
        @pl.when(dist == 2)
        def _():
            spread_half(0)
            spread_half(1)

    def relayed(i, e):
        return lax.rem(x - (core * 2 + e) + 4, 4) == 1 + 2 * i

    def relay(step):
        i = order(step)
        for e in range(2):

            @pl.when(relayed(i, e))
            def _():
                for c2 in range(2):
                    which = e * 2 + c2
                    landed(place(i, which), x2r.at[which, i])
                    to_x(i, place(i, which), which, x3s.at[which, i], 1 - 2 * i, core)

    def arrive():
        for i in range(2):
            for e in range(2):

                @pl.when(jnp.logical_not(relayed(i, e)))
                def _():
                    for c2 in range(2):
                        landed(place(i, e * 2 + c2), x2r.at[e * 2 + c2, i])

    for k in range(4):
        for h in range(2):
            pass_on_z(panel_base(k, h), 64, z1s.at[k, h], z1r.at[k, h])
    spread_near(0)
    for k in range(4):
        for h in range(2):
            base = panel_base(k, h)
            opposite_z(base, 64, z1r.at[k, h])
            part = s_ref.at[:, pl.ds(base, 64)]
            remote(part, part, d1s.at[k, h], d1r.at[k, h], sibling, across)
    pass_on(xm, 16, xms, xmr, along_x)
    spread_near(1)
    opposite(xm, 16, xmr)
    for h in range(2):
        dx = lax.rem(lax.rem(q, 2) * 2 + h - x + 4, 4)
        mp_ref[pl.ds(mrow, 32), h * 512 : (h + 1) * 512] = pick(dx, pm[...], [xm[i] for i in range(3)])
    part = mp_ref.at[pl.ds(mrow, 32)]
    remote(part, part, dms.at[0], dmr.at[0], sibling, across)
    for copy in across:
        copy.wait_recv()

    def drain():
        for copy in sent + across:
            copy.wait_send()
        for i in range(2):

            @pl.when(dist == 0)
            def _():
                for j in range(2):
                    landed(half_of(i), y2s.at[i, j])

            @pl.when(dist == 1 + 2 * i)
            def _():
                landed(half_of(i), y2s.at[i, 1 - i])

            for j in range(2):
                landed(half_of(i), x2s.at[i, j])

            @pl.when(core != target)
            def _():
                landed(half_of(i), x2s.at[i, 2])

            for e in range(2):

                @pl.when(relayed(i, e))
                def _():
                    for c2 in range(2):
                        landed(place(i, e * 2 + c2), x3s.at[e * 2 + c2, i])

    return spread_far, relay, arrive, drain


def on_device(genotypes, frequencies, trait_scores, typed_mask, panel_index):
    dma = pltpu.SemaphoreType.DMA
    hbm, vmem = pl.BlockSpec(memory_space=pltpu.HBM), pl.BlockSpec(memory_space=pltpu.VMEM)
    own = eliminate_scratch()
    gathered = [
        pltpu.VMEM((512, 512), jnp.int32),
        pltpu.VMEM((1, 512), f32),
        pltpu.VMEM((traits, 512), f32),
        pltpu.VMEM((1, 512), jnp.int32),
        pltpu.VMEM((4, C0 + nc, 512), bf16),
        pltpu.VMEM((traits, n), f32),
        pltpu.VMEM((traits, 512), f32),
        pltpu.VMEM((512, 512), bf16),
        *[pltpu.VMEM((3, 64, 512), bf16)] * 4,
        pltpu.VMEM((4, 64, 512), bf16),
        *[pltpu.VMEM((3, 64, 512), bf16)] * 4,
        pltpu.VMEM((3, 32, 512), f32),
        pltpu.VMEM((32, 512), f32),
        pltpu.VMEM((3, 32, 512), f32),
        pltpu.VMEM((4, 256, 512), bf16),
    ]
    sems = [dma(shape) for shape in (
        (4,), (4, 4), (4, 4), (4, 4), (4, 4), (4, 2, 4), (4, 2, 4), (4, 2), (4, 2), (4,), (4,), (1,), (1,),
        (2, 2), (2,), (2, 3), (4, 2), (4, 2), (4,), (4,), (4,), (4,), (1,), (1,))]

    def kernel(g, f, tr, tm, panel_ref, cond_ref, whit_ref, res_ref, *rest):
        work, rest = rest[: len(own)], rest[len(own) :]
        bufs, rest = rest[: len(gathered)], rest[len(gathered) :]
        s_ref, mp_ref, mk_ref = bufs[4], bufs[5], bufs[6]
        yb, xb = bufs[8:12], bufs[13:17]

        def meanwhile():
            for ref in work[2:5]:
                ref[...] = jnp.zeros_like(ref)

        spread_far, relay, arrive, drain = gather(
            (g, f, tr, tm), panel_ref, *bufs[:8], yb, bufs[12], xb, *bufs[17:], rest, meanwhile)
        steps = {(0, 0): spread_far, (2, 0): lambda: relay(0), (4, 0): lambda: relay(1), (8, 0): arrive}

        def service(b, part):
            steps.get((b, part), lambda: None)()

        eliminate(lax.rem(panel_ref[0], 8), lax.axis_index("row") * 512, lax.axis_index("col") * 1024,
                  s_ref, mp_ref, mk_ref, cond_ref, whit_ref, res_ref, *work, service=service)
        drain()

    return pl.pallas_call(
        kernel,
        out_shape=(
            jax.ShapeDtypeStruct((nr, nc), f32),
            jax.ShapeDtypeStruct((traits, n), f32),
            jax.ShapeDtypeStruct((traits, nr), f32),
        ),
        in_specs=[hbm] * 4 + [pl.BlockSpec(memory_space=pltpu.SMEM)],
        out_specs=(vmem,) * 3,
        scratch_shapes=own + gathered + sems,
        compiler_params=pltpu.CompilerParams(vmem_limit_bytes=44 * 1024 * 1024, collective_id=0, has_side_effects=True),
    )(*(pltpu.with_memory_space_constraint(a, pltpu.HBM) for a in (genotypes, frequencies[None, :], trait_scores, typed_mask[None, :])), panel_index)


def solution(mesh):
    placed = (P("samp", "row"), P("row"), P(None, "row"), P("row"), P())
    return jax.shard_map(
        on_device,
        mesh=mesh,
        in_specs=placed,
        out_specs=(P("row", "col"), P(), P(None, "row")),
        check_vma=False,
    )
```

```python
import functools

import jax
import jax.numpy as jnp
from jax import lax
from jax.experimental import pallas as pl
from jax.experimental.pallas import tpu as pltpu
from jax.sharding import PartitionSpec as P

MESH = pl.DeviceIdType.MESH

ridge = 0.1
NT = (((1,), (1,)), ((), ()))
TN = (((0,), (0,)), ((), ()))
f32, bf16 = jnp.float32, jnp.bfloat16
n, nr, nc, traits, samples = 1024, 512, 1024, 64, 2048
R0, C0 = n, n + nr
T0 = n + nr
I0 = T0 + traits


def split2(x):
    h = x.astype(bf16)
    return h, (x - h.astype(f32)).astype(bf16)


def split3(x):
    h = x.astype(bf16)
    r = x - h.astype(f32)
    m = r.astype(bf16)
    return h, m, (r - m.astype(f32)).astype(bf16)


dot = functools.partial(lax.dot_general, dimension_numbers=NT, preferred_element_type=f32)


def spread(x, i, k):
    return jnp.broadcast_to(x[i : i + 1, k : k + 1], (8, 128))


def twice(x):
    return jnp.concatenate([x, x], axis=1)


def eight(x_ref, at, a, rows, below):
    cols, pairs, extra = below
    for k in range(8):
        r = lax.rsqrt(a[k, k])
        rec = r * r
        if k < 7:
            square = a[k + 1, k] * a[k + 1, k]
        m = {i: a[i, k] * rec for i in range(k + 1, 8)}
        for i in range(k + 1, 8):
            for j in range(k + 1, i + 1):
                if i == j == k + 1:
                    a[i, j] = a[i, j] - square * rec
                else:
                    a[i, j] = a[i, j] - m[i] * a[j, k]
        for i in range(k + 1, 8):
            rows[i] = rows[i] - twice(m[i]) * rows[k]
            if extra:
                extra[i] = extra[i] - m[i] * extra[k]
        if cols:
            m2 = cols[k] * rec
            for j in range(k + 1, 8):
                cols[j] = cols[j] - m2 * a[j, k]
            pairs[0] = pairs[0] - twice(m2) * rows[k]
            pairs[1] = pairs[1] - m2 * extra[k]
        x_ref[pl.ds(at + k, 1), :] = (rows[k] * twice(r))[:1]


def pivots(x_ref, t):
    j0 = pl.multiple_of(t * 16, 16)
    block = pltpu.roll(x_ref[pl.ds(j0, 16), :128], lax.rem(128 - j0, 128), 1)
    top, low = block[:8], block[8:]
    rows = [jnp.broadcast_to(x_ref[pl.ds(j0 + i, 1), :], (8, 256)) for i in range(8)]
    a = {(i, k): spread(top, i, k) for i in range(8) for k in range(i + 1)}
    cols = [jnp.broadcast_to(low[:, k : k + 1], (8, 128)) for k in range(8)]
    extra = [jnp.broadcast_to(top[i : i + 1], (8, 128)) for i in range(8)]
    pairs = [x_ref[pl.ds(j0 + 8, 8), :], low]
    eight(x_ref, j0, a, rows, (cols, pairs, extra))
    rows = [jnp.broadcast_to(pairs[0][i : i + 1], (8, 256)) for i in range(8)]
    a = {(i, k): spread(pairs[1], i, 8 + k) for i in range(8) for k in range(i + 1)}
    eight(x_ref, j0 + 8, a, rows, (None, None, None))


def update(x_ref, t):
    j0 = pl.multiple_of(t * 16, 16)
    u = x_ref[pl.ds(j0, 16), :]
    h, m, l = split3(u)
    rhs = jnp.concatenate([h, m, h, l, h, m], axis=0)
    left = jnp.concatenate([h, h, m, h, l, m], axis=0)[:, :128].astype(f32)
    lane = lax.broadcasted_iota(jnp.int32, left.shape, 1)
    left = jnp.where(lane >= j0 + 16, left, 0.0).astype(bf16)
    x_ref[...] = x_ref[...] - lax.dot_general(left, rhs, TN, preferred_element_type=f32)


def joined(ref, rows, lanes):
    h, l = ref[0][rows, lanes], ref[1][rows, lanes]
    return jnp.concatenate([h, h, l], axis=1), jnp.concatenate([h, l, h], axis=1)


def eliminate(panel, rows_at, cols_at, s_ref, mask_p_ref, mask_r_ref, cond_ref, whit_ref, res_ref,
              x_ref, w_ref, hi_ref, lo_ref, g_ref, h_ref, service=lambda b, part: None):
    both = (hi_ref, lo_ref)
    iota = functools.partial(lax.broadcasted_iota, jnp.int32)
    eye = (iota((128, 128), 0) == iota((128, 128), 1)).astype(f32)

    def block(b):
        return slice(b * 128, (b + 1) * 128)

    def start(b):
        w = w_ref.at[b % 2]
        w[b * 128 : R0, :] = jnp.zeros((R0 - b * 128, 128), f32)
        w[block(b), :] = eye * ridge
        ids = iota((nr, 128), 0) + (rows_at - panel * n - b * 128)
        w[R0:T0, :] = jnp.where(ids == iota((nr, 128), 1), ridge, 0.0)
        w[T0:I0, :] = jnp.zeros((traits, 128), f32)
        if b:
            w[I0 : I0 + b * 128, :] = jnp.zeros((b * 128, 128), f32)
        w[I0 + b * 128 : I0 + (b + 1) * 128, :] = eye

    start(0)
    acc = dot(s_ref[0, :T0, :], s_ref[0, :128, :])
    for g in range(1, 4):
        acc = acc + dot(s_ref[g, :T0, :], s_ref[g, :128, :])
    w_ref[0, :T0, :] = w_ref[0, :T0, :] + acc * (1.0 / samples)

    for b in range(8):
        service(b, 0)
        now, later = w_ref.at[b % 2], w_ref.at[(b + 1) % 2]
        x_ref[:, :128] = now[block(b), :]
        x_ref[:, 128:] = eye
        low, high = (b + 1) * 128, I0 + (b + 1) * 128
        rows = slice(low, high)
        if b < 7:
            start(b + 1)

        def body(t, earlier):
            pivots(x_ref, t)
            if b < 7:
                lanes = pl.ds(pl.multiple_of(lax.rem(t, 2) * 256, 256), 256)
                new = dot(s_ref[t // 2, low:T0, lanes], s_ref[t // 2, low : low + 128, lanes]) * (1.0 / samples)
                if earlier:
                    lanes = pl.ds(pl.multiple_of(t * 128, 128), 128)
                    taken = dot(joined(both, rows, lanes)[0], joined(both, slice(low, low + 128), lanes)[1])
                    later[low:T0, :] = later[low:T0, :] + (new - taken[: T0 - low])
                    later[T0:high, :] = later[T0:high, :] - taken[T0 - low :]
                else:
                    later[low:T0, :] = later[low:T0, :] + new
            if earlier:
                lanes = block(b - 1)
                to = pl.ds(pl.multiple_of(t * 128, 128), 128)
                right = joined(both, pl.ds(pl.multiple_of(I0 + t * 128, 64), 128), lanes)[1]
                g_ref[:, to] = g_ref[:, to] + dot(joined(both, slice(R0, T0), lanes)[0], right)
            update(x_ref, t)

        if b:
            pl.loop(0, b)(functools.partial(body, earlier=True))
        if b == 0:
            pl.loop(0, 4)(functools.partial(body, earlier=False))
        service(b, 1)
        pl.loop(b or 4, 8)(functools.partial(body, earlier=False))
        service(b, 2)
        now[T0:I0, :] = now[T0:I0, :] + mask_p_ref[:, block(b)]
        inv_h, inv_l = split2(x_ref[:, 128:])
        wh, wl = split2(now[rows, :])
        out = dot(jnp.concatenate([wh, wh, wl], axis=1), jnp.concatenate([inv_h, inv_l, inv_h], axis=1))
        h, l = split2(out)
        hi_ref[rows, block(b)] = h
        lo_ref[rows, block(b)] = l
        whit_ref[:, block(b)] = out[T0 - low : I0 - low]
        if b < 7:
            later[rows, :] = later[rows, :] - dot(jnp.concatenate([h, h, l], axis=1), jnp.concatenate([h, l, h], axis=1)[:128])

    left = joined(both, slice(R0, T0), block(7))[0]
    g_ref[...] = g_ref[...] + dot(left, joined(both, slice(I0, I0 + n), block(7))[1])

    @pl.loop(0, 4)
    def _(g):
        gh, gl = split2(g_ref[...])
        taken = jnp.dot(gh, s_ref[g, :n, :], preferred_element_type=f32) + jnp.dot(gl, s_ref[g, :n, :], preferred_element_type=f32)
        h_ref[g] = (s_ref[g, R0:C0, :].astype(f32) - taken).astype(bf16)

    service(8, 0)
    same = jnp.where(cols_at == panel * n, ridge, 0.0)

    @pl.loop(0, 4)
    def _(j):
        at = pl.multiple_of(j * 256, 256)
        acc = dot(h_ref[0], s_ref[0, pl.ds(C0 + at, 256), :])
        for g in range(1, 4):
            acc = acc + dot(h_ref[g], s_ref[g, pl.ds(C0 + at, 256), :])
        ids = iota((nr, 256), 0) + (rows_at - cols_at - at)
        acc = acc * (1.0 / samples) + jnp.where(ids == iota((nr, 256), 1), ridge, 0.0)
        cond_ref[:, pl.ds(at, 256)] = acc - same * g_ref[:, pl.ds(at, 256)]

    th, tl = hi_ref[T0:I0, :], lo_ref[T0:I0, :]
    rh, rl = hi_ref[R0:T0, :], lo_ref[R0:T0, :]
    res_ref[...] = mask_r_ref[...] - (dot(th, rh) + dot(th, rl) + dot(tl, rh))


def eliminate_scratch():
    return [
        pltpu.VMEM((128, 256), f32),
        pltpu.VMEM((2, I0 + n, 128), f32),
        pltpu.VMEM((I0 + n, n), bf16),
        pltpu.VMEM((I0 + n, n), bf16),
        pltpu.VMEM((nr, n), f32),
        pltpu.VMEM((4, nr, samples // 4), bf16),
    ]


def gather(ins, panel_ref, g_ref, f_ref, tr_ref, tm_ref, s_ref, mp_ref, mk_ref, own_ref, yb, pp, xb, ym, pm, xm, yc, sems, meanwhile):
    (ins_sem, y1s, y1r, x1s, x1r, z1s, z1r, d1s, d1r, z0s, z0r, d0s, d0r, y2s, y2r, x2s, x2r, x3s, yms, ymr, xms, xmr, dms, dmr) = sems
    s = lax.axis_index("samp")
    r = lax.axis_index("row")
    c = lax.axis_index("col")
    y, x = r // 4, lax.rem(r, 4)
    zh, core = c // 2, lax.rem(c, 2)
    q = lax.rem(panel_ref[0], 8)

    def at(dy=0, dx=0, dz=0, core_to=None):
        ny = lax.rem(y + dy + 4, 4)
        nx = lax.rem(x + dx + 4, 4)
        nz = lax.rem(zh * 4 + s + dz + 16, 16)
        k = core if core_to is None else core_to
        return (lax.rem(nz, 4), ny * 4 + nx, nz // 4 * 2 + k)

    loads = [pltpu.make_async_copy(src, dst, ins_sem.at[i]) for i, (src, dst) in enumerate(zip(ins, (g_ref, f_ref, tr_ref, tm_ref)))]
    for load in loads:
        load.start()
    sibling = at(core_to=1 - core)
    sent, across = [], []

    def remote(src, dst, send, recv, to, kept=sent):
        copy = pltpu.make_async_remote_copy(src_ref=src, dst_ref=dst, send_sem=send, recv_sem=recv, device_id=to, device_id_type=MESH)
        copy.start()
        kept.append(copy)

    def landed(ref, sem):
        pltpu.make_async_copy(ref, ref, sem).wait()

    barrier = pltpu.get_barrier_semaphore()
    partners = [at(dy=d) for d in (-1, 1)]
    partners += [at(dx=d, core_to=k) for d in (-1, 1) for k in (0, 1)]
    partners += [at(dz=d) for d in (-1, 1)] + [sibling]
    for to in partners:
        pl.semaphore_signal(barrier, inc=1, device_id=to, device_id_type=MESH)
    for load in loads:
        load.wait()
    freq = f_ref[...]
    spread = jnp.sqrt(2.0 * freq * (1.0 - freq))

    def standardize(k):
        lanes = slice(k * 128, (k + 1) * 128)
        value = (g_ref[:, lanes].astype(f32) - 2.0 * freq[:, lanes]) / spread[:, lanes]
        own_ref[lanes, :] = value.T.astype(bf16)

    standardize(0)
    pl.semaphore_wait(barrier, len(partners))

    half = pl.multiple_of(core * 256, 256)
    mrow = pl.multiple_of(core * 32, 32)
    def send(src, slots, ss, rs, ways):
        for i in range(2):
            remote(src, slots.at[i], ss.at[i], rs.at[i], ways[i])

    def pass_on(slots, size, ss, rs, ways):
        for i in range(2):
            landed(slots.at[i], rs.at[i])
            part = pl.ds(i * size, size)
            remote(slots.at[i, part], slots.at[2, part], ss.at[2 + i], rs.at[2 + i], ways[i])

    def opposite(slots, size, rs):
        for i in range(2):
            landed(slots.at[2, pl.ds(i * size, size)], rs.at[2 + i])

    def pick(distance, mine, slots):
        out = jnp.where(distance == 1, slots[1], mine)
        out = jnp.where(distance == 3, slots[0], out)
        return jnp.where(distance == 2, slots[2], out)

    along_y, along_x = (at(dy=1), at(dy=-1)), (at(dx=1), at(dx=-1))
    along_z = (at(dz=1), at(dz=-1))
    def send_y(k):
        send(own_ref.at[pl.ds(pl.multiple_of(k * 128 + core * 64, 64), 64)], yb[k], y1s.at[k], y1r.at[k], along_y)

    send_y(0)
    standardize(1)
    send_y(1)
    standardize(2)
    standardize(3)

    def send_z(src, base, size, ss, rs):
        for i in range(2):
            remote(src, s_ref.at[s, pl.ds(base, size)], ss.at[i], rs.at[i], along_z[i])

    def pass_on_z(base, size, ss, rs):
        for i in range(2):
            group = lax.rem(s + (3 if i == 0 else 1), 4)
            landed(s_ref.at[group, pl.ds(base, size)], rs.at[i])
            part = s_ref.at[group, pl.ds(pl.multiple_of(base + i * size // 2, 32), size // 2)]
            remote(part, part, ss.at[2 + i], rs.at[2 + i], along_z[i])

    def opposite_z(base, size, rs):
        for i in range(2):
            landed(s_ref.at[lax.rem(s + 2, 4), pl.ds(pl.multiple_of(base + i * size // 2, 32), size // 2)], rs.at[2 + i])

    row_base = pl.multiple_of(n + half, 256)
    send_z(own_ref.at[pl.ds(half, 256)], row_base, 256, z0s, z0r)
    s_ref[s, pl.ds(row_base, 256), :] = own_ref[pl.ds(half, 256), :]
    mk_ref[...] = tr_ref[...] * tm_ref[...].astype(f32)
    dy = lax.rem(q // 2 - y + 4, 4)

    def panel_base(k, h):
        return pl.multiple_of(h * 512 + k * 128 + core * 64, 64)

    def turn_x(k):
        opposite(yb[k], 32, y1r.at[k])
        mine = own_ref[pl.ds(pl.multiple_of(k * 128 + core * 64, 64), 64), :]
        pp[k, :, :] = pick(dy, mine, [yb[k][i] for i in range(3)])
        send(pp.at[k], xb[k], x1s.at[k], x1r.at[k], along_x)

    def turn_z(k):
        opposite(xb[k], 32, x1r.at[k])
        for h in range(2):
            dx = lax.rem(lax.rem(q, 2) * 2 + h - x + 4, 4)
            base = panel_base(k, h)
            s_ref[s, pl.ds(base, 64), :] = pick(dx, pp[k], [xb[k][i] for i in range(3)])
            send_z(s_ref.at[s, pl.ds(base, 64)], base, 64, z1s.at[k, h], z1r.at[k, h])

    def forward_z(k):
        for h in range(2):
            pass_on_z(panel_base(k, h), 64, z1s.at[k, h], z1r.at[k, h])

    def turn_core(k):
        for h in range(2):
            base = panel_base(k, h)
            opposite_z(base, 64, z1r.at[k, h])
            part = s_ref.at[:, pl.ds(base, 64)]
            remote(part, part, d1s.at[k, h], d1r.at[k, h], sibling, across)

    def forward_y(k):
        pass_on(yb[k], 32, y1s.at[k], y1r.at[k], along_y)
        if k < 2:
            send_y(k + 2)

    stages = (
        forward_y,
        turn_x,
        lambda k: pass_on(xb[k], 32, x1s.at[k], x1r.at[k], along_x),
        turn_z,
        forward_z,
        turn_core,
    )

    def wave(step):
        for behind in reversed(range(len(stages))):
            if 0 <= step - behind < 4:
                stages[behind](step - behind)

    wave(0)
    wave(1)
    send(mk_ref.at[pl.ds(mrow, 32)], ym, yms, ymr, along_y)
    meanwhile()
    pass_on_z(row_base, 256, z0s, z0r)
    wave(2)
    wave(3)
    pass_on(ym, 16, yms, ymr, along_y)
    wave(4)
    opposite_z(row_base, 256, z0r)
    mine = s_ref.at[:, pl.ds(row_base, 256)]
    remote(mine, mine, d0s.at[0], d0r.at[0], sibling, across)

    dist = lax.rem(y - zh + 4, 4)
    target = x // 2
    slot = lax.rem(x, 2) * 2 + core

    def half_of(i):
        return yc.at[pl.ds(2 * i, 2)]

    def to_y(i, src, sem, dy):
        pltpu.make_async_remote_copy(src_ref=src, dst_ref=half_of(i), send_sem=sem, recv_sem=y2r.at[i], device_id=at(dy=dy),
                                     device_id_type=MESH).start()

    @pl.when(dist == 0)
    def _():
        parts = [s_ref.at[2 * i : 2 * i + 2, pl.ds(row_base, 256)] for i in range(2)]
        for i, dy in ((0, 1), (1, -1), (1, 1), (0, -1)):
            to_y(i, parts[i], y2s.at[i, (dy + 1) // 2], dy)
        for i in range(2):
            pltpu.make_async_copy(parts[i], half_of(i), y2r.at[i]).start()

    opposite(ym, 16, ymr)
    pm[...] = pick(dy, mk_ref[pl.ds(mrow, 32), :], [ym[i] for i in range(3)])
    send(pm, xm, xms, xmr, along_x)

    def place(i, which):
        return s_ref.at[pl.ds(2 * i, 2), pl.ds(pl.multiple_of(n + nr + which * 256, 256), 256)]

    def to_x(i, src, which, sem, dx, k):
        pltpu.make_async_remote_copy(src_ref=src, dst_ref=place(i, which), send_sem=sem, recv_sem=x2r.at[which, i],
                                     device_id=at(dx=dx, core_to=k), device_id_type=MESH).start()

    def order(step):
        return jnp.where(dist == 3, 1 - step, step)

    def spread_half(step):
        i = order(step)
        landed(half_of(i), y2r.at[i])
        if step == 0:

            @pl.when(dist == 1)
            def _():
                to_y(0, half_of(0), y2s.at[0, 1], 1)

            @pl.when(dist == 3)
            def _():
                to_y(1, half_of(1), y2s.at[1, 0], -1)

        for dx in (1, -1):
            to_x(i, half_of(i), slot, x2s.at[i, (dx + 1) // 2], dx, target)

        @pl.when(core == target)
        def _():
            pltpu.make_async_copy(half_of(i), place(i, slot), x2r.at[slot, i]).start()

        @pl.when(core != target)
        def _():
            to_x(i, half_of(i), slot, x2s.at[i, 2], 0, 1 - core)

    def spread_near(step):
        @pl.when(dist != 2)
        def _():
            spread_half(step)

    def spread_far(step):
        @pl.when(dist == 2)
        def _():
            spread_half(step)

    def relayed(i, e):
        return lax.rem(x - (core * 2 + e) + 4, 4) == 1 + 2 * i

    def relay(step):
        i = order(step)
        for e in range(2):

            @pl.when(relayed(i, e))
            def _():
                for c2 in range(2):
                    which = e * 2 + c2
                    landed(place(i, which), x2r.at[which, i])
                    to_x(i, place(i, which), which, x3s.at[which, i], 1 - 2 * i, core)

    def arrive():
        for i in range(2):
            for e in range(2):

                @pl.when(jnp.logical_not(relayed(i, e)))
                def _():
                    for c2 in range(2):
                        landed(place(i, e * 2 + c2), x2r.at[e * 2 + c2, i])

    wave(5)
    wave(6)
    pass_on(xm, 16, xms, xmr, along_x)
    wave(7)
    spread_near(0)
    wave(8)
    for copy in across:
        copy.wait_recv()

    def scores(step):
        part = mp_ref.at[pl.ds(mrow, 32)]
        if step == 0:
            opposite(xm, 16, xmr)
            for h in range(2):
                dx = lax.rem(lax.rem(q, 2) * 2 + h - x + 4, 4)
                mp_ref[pl.ds(mrow, 32), h * 512 : (h + 1) * 512] = pick(dx, pm[...], [xm[i] for i in range(3)])
            remote(part, part, dms.at[0], dmr.at[0], sibling)
        else:
            landed(part, dmr.at[0])

    def drain():
        for copy in sent + across:
            copy.wait_send()
        for i in range(2):

            @pl.when(dist == 0)
            def _():
                for j in range(2):
                    landed(half_of(i), y2s.at[i, j])

            @pl.when(dist == 1 + 2 * i)
            def _():
                landed(half_of(i), y2s.at[i, 1 - i])

            for j in range(2):
                landed(half_of(i), x2s.at[i, j])

            @pl.when(core != target)
            def _():
                landed(half_of(i), x2s.at[i, 2])

            for e in range(2):

                @pl.when(relayed(i, e))
                def _():
                    for c2 in range(2):
                        landed(place(i, e * 2 + c2), x3s.at[e * 2 + c2, i])

    return spread_near, spread_far, relay, arrive, scores, drain


def on_device(genotypes, frequencies, trait_scores, typed_mask, panel_index):
    dma = pltpu.SemaphoreType.DMA
    hbm, vmem = pl.BlockSpec(memory_space=pltpu.HBM), pl.BlockSpec(memory_space=pltpu.VMEM)
    own = eliminate_scratch()
    gathered = [
        pltpu.VMEM((512, 512), jnp.int32),
        pltpu.VMEM((1, 512), f32),
        pltpu.VMEM((traits, 512), f32),
        pltpu.VMEM((1, 512), jnp.int32),
        pltpu.VMEM((4, C0 + nc, 512), bf16),
        pltpu.VMEM((traits, n), f32),
        pltpu.VMEM((traits, 512), f32),
        pltpu.VMEM((512, 512), bf16),
        *[pltpu.VMEM((3, 64, 512), bf16)] * 4,
        pltpu.VMEM((4, 64, 512), bf16),
        *[pltpu.VMEM((3, 64, 512), bf16)] * 4,
        pltpu.VMEM((3, 32, 512), f32),
        pltpu.VMEM((32, 512), f32),
        pltpu.VMEM((3, 32, 512), f32),
        pltpu.VMEM((4, 256, 512), bf16),
    ]
    sems = [dma(shape) for shape in (
        (4,), (4, 4), (4, 4), (4, 4), (4, 4), (4, 2, 4), (4, 2, 4), (4, 2), (4, 2), (4,), (4,), (1,), (1,),
        (2, 2), (2,), (2, 3), (4, 2), (4, 2), (4,), (4,), (4,), (4,), (1,), (1,))]

    def kernel(g, f, tr, tm, panel_ref, cond_ref, whit_ref, res_ref, *rest):
        work, rest = rest[: len(own)], rest[len(own) :]
        bufs, rest = rest[: len(gathered)], rest[len(gathered) :]
        s_ref, mp_ref, mk_ref = bufs[4], bufs[5], bufs[6]
        yb, xb = bufs[8:12], bufs[13:17]

        def meanwhile():
            for ref in work[2:4]:
                ref[I0:, :] = jnp.zeros((n, n), bf16)
            work[4][...] = jnp.zeros((nr, n), f32)

        spread_near, spread_far, relay, arrive, scores, drain = gather(
            (g, f, tr, tm), panel_ref, *bufs[:8], yb, bufs[12], xb, *bufs[17:], rest, meanwhile)
        steps = {(0, 1): (lambda: scores(0),), (0, 2): (lambda: scores(1),),
                 (1, 0): (lambda: spread_near(1), lambda: spread_far(0)), (2, 0): (lambda: spread_far(1),),
                 (4, 0): (lambda: relay(0),), (6, 0): (lambda: relay(1),), (8, 0): (arrive,)}

        def service(b, part):
            for step in steps.get((b, part), ()):
                step()

        eliminate(lax.rem(panel_ref[0], 8), lax.axis_index("row") * 512, lax.axis_index("col") * 1024,
                  s_ref, mp_ref, mk_ref, cond_ref, whit_ref, res_ref, *work, service=service)
        drain()

    return pl.pallas_call(
        kernel,
        out_shape=(
            jax.ShapeDtypeStruct((nr, nc), f32),
            jax.ShapeDtypeStruct((traits, n), f32),
            jax.ShapeDtypeStruct((traits, nr), f32),
        ),
        in_specs=[hbm] * 4 + [pl.BlockSpec(memory_space=pltpu.SMEM)],
        out_specs=(vmem,) * 3,
        scratch_shapes=own + gathered + sems,
        compiler_params=pltpu.CompilerParams(vmem_limit_bytes=44 * 1024 * 1024, collective_id=0, has_side_effects=True),
    )(*(pltpu.with_memory_space_constraint(a, pltpu.HBM) for a in (genotypes, frequencies[None, :], trait_scores, typed_mask[None, :])), panel_index)


def solution(mesh):
    placed = (P("samp", "row"), P("row"), P(None, "row"), P("row"), P())
    return jax.shard_map(
        on_device,
        mesh=mesh,
        in_specs=placed,
        out_specs=(P("row", "col"), P(), P(None, "row")),
        check_vma=False,
    )
```

```python
import functools

import jax
import jax.numpy as jnp
from jax import lax
from jax.experimental import pallas as pl
from jax.experimental.pallas import tpu as pltpu
from jax.sharding import PartitionSpec as P

MESH = pl.DeviceIdType.MESH

ridge = 0.1
NT = (((1,), (1,)), ((), ()))
TN = (((0,), (0,)), ((), ()))
f32, bf16 = jnp.float32, jnp.bfloat16
n, nr, nc, traits, samples = 1024, 512, 1024, 64, 2048
R0, C0 = n, n + nr
T0 = n + nr
I0 = T0 + traits


def split2(x):
    h = x.astype(bf16)
    return h, (x - h.astype(f32)).astype(bf16)


def split3(x):
    h = x.astype(bf16)
    r = x - h.astype(f32)
    m = r.astype(bf16)
    return h, m, (r - m.astype(f32)).astype(bf16)


dot = functools.partial(lax.dot_general, dimension_numbers=NT, preferred_element_type=f32)


def spread(x, i, k):
    return jnp.broadcast_to(x[i : i + 1, k : k + 1], (8, 128))


def twice(x):
    return jnp.concatenate([x, x], axis=1)


def eight(x_ref, at, a, rows, below):
    cols, pairs, extra = below
    for k in range(8):
        r = lax.rsqrt(a[k, k])
        rec = r * r
        if k < 7:
            square = a[k + 1, k] * a[k + 1, k]
        m = {i: a[i, k] * rec for i in range(k + 1, 8)}
        for i in range(k + 1, 8):
            for j in range(k + 1, i + 1):
                if i == j == k + 1:
                    a[i, j] = a[i, j] - square * rec
                else:
                    a[i, j] = a[i, j] - m[i] * a[j, k]
        for i in range(k + 1, 8):
            rows[i] = rows[i] - twice(m[i]) * rows[k]
            if extra:
                extra[i] = extra[i] - m[i] * extra[k]
        if cols:
            m2 = cols[k] * rec
            for j in range(k + 1, 8):
                cols[j] = cols[j] - m2 * a[j, k]
            pairs[0] = pairs[0] - twice(m2) * rows[k]
            pairs[1] = pairs[1] - m2 * extra[k]
        x_ref[pl.ds(at + k, 1), :] = (rows[k] * twice(r))[:1]


def pivots(x_ref, t):
    j0 = pl.multiple_of(t * 16, 16)
    block = pltpu.roll(x_ref[pl.ds(j0, 16), :128], lax.rem(128 - j0, 128), 1)
    top, low = block[:8], block[8:]
    rows = [jnp.broadcast_to(x_ref[pl.ds(j0 + i, 1), :], (8, 256)) for i in range(8)]
    a = {(i, k): spread(top, i, k) for i in range(8) for k in range(i + 1)}
    cols = [jnp.broadcast_to(low[:, k : k + 1], (8, 128)) for k in range(8)]
    extra = [jnp.broadcast_to(top[i : i + 1], (8, 128)) for i in range(8)]
    pairs = [x_ref[pl.ds(j0 + 8, 8), :], low]
    eight(x_ref, j0, a, rows, (cols, pairs, extra))
    rows = [jnp.broadcast_to(pairs[0][i : i + 1], (8, 256)) for i in range(8)]
    a = {(i, k): spread(pairs[1], i, 8 + k) for i in range(8) for k in range(i + 1)}
    eight(x_ref, j0 + 8, a, rows, (None, None, None))


def update(x_ref, t):
    j0 = pl.multiple_of(t * 16, 16)
    u = x_ref[pl.ds(j0, 16), :]
    h, m, l = split3(u)
    rhs = jnp.concatenate([h, m, h, l, h, m], axis=0)
    left = jnp.concatenate([h, h, m, h, l, m], axis=0)[:, :128].astype(f32)
    lane = lax.broadcasted_iota(jnp.int32, left.shape, 1)
    left = jnp.where(lane >= j0 + 16, left, 0.0).astype(bf16)
    x_ref[...] = x_ref[...] - lax.dot_general(left, rhs, TN, preferred_element_type=f32)


def joined(ref, rows, lanes):
    h, l = ref[0][rows, lanes], ref[1][rows, lanes]
    return jnp.concatenate([h, h, l], axis=1), jnp.concatenate([h, l, h], axis=1)


def eliminate(panel, rows_at, cols_at, s_ref, mask_p_ref, mask_r_ref, cond_ref, whit_ref, res_ref,
              x_ref, w_ref, hi_ref, lo_ref, g_ref, h_ref, service=lambda b, part: None):
    both = (hi_ref, lo_ref)
    iota = functools.partial(lax.broadcasted_iota, jnp.int32)
    eye = (iota((128, 128), 0) == iota((128, 128), 1)).astype(f32)

    def block(b):
        return slice(b * 128, (b + 1) * 128)

    def start(b):
        w = w_ref.at[b % 2]
        w[b * 128 : R0, :] = jnp.zeros((R0 - b * 128, 128), f32)
        w[block(b), :] = eye * ridge
        ids = iota((nr, 128), 0) + (rows_at - panel * n - b * 128)
        w[R0:T0, :] = jnp.where(ids == iota((nr, 128), 1), ridge, 0.0)
        w[T0:I0, :] = jnp.zeros((traits, 128), f32)
        if b:
            w[I0 : I0 + b * 128, :] = jnp.zeros((b * 128, 128), f32)
        w[I0 + b * 128 : I0 + (b + 1) * 128, :] = eye

    ids = iota((nr, 128), 0) + (rows_at - panel * n)
    w_ref[0, :128, :] = w_ref[0, :128, :] + eye * ridge
    w_ref[0, R0:T0, :] = w_ref[0, R0:T0, :] + jnp.where(ids == iota((nr, 128), 1), ridge, 0.0)
    w_ref[0, T0:I0, :] = jnp.zeros((traits, 128), f32)
    w_ref[0, I0 : I0 + 128, :] = eye

    for b in range(8):
        service(b, 0)
        now, later = w_ref.at[b % 2], w_ref.at[(b + 1) % 2]
        x_ref[:, :128] = now[block(b), :]
        x_ref[:, 128:] = eye
        low, high = (b + 1) * 128, I0 + (b + 1) * 128
        rows = slice(low, high)
        if b < 7:
            start(b + 1)

        def body(t, earlier):
            pivots(x_ref, t)
            if b < 7:
                lanes = pl.ds(pl.multiple_of(lax.rem(t, 2) * 256, 256), 256)
                new = dot(s_ref[t // 2, low:T0, lanes], s_ref[t // 2, low : low + 128, lanes]) * (1.0 / samples)
                if earlier:
                    lanes = pl.ds(pl.multiple_of(t * 128, 128), 128)
                    taken = dot(joined(both, rows, lanes)[0], joined(both, slice(low, low + 128), lanes)[1])
                    later[low:T0, :] = later[low:T0, :] + (new - taken[: T0 - low])
                    later[T0:high, :] = later[T0:high, :] - taken[T0 - low :]
                else:
                    later[low:T0, :] = later[low:T0, :] + new
            if earlier:
                lanes = block(b - 1)
                to = pl.ds(pl.multiple_of(t * 128, 128), 128)
                right = joined(both, pl.ds(pl.multiple_of(I0 + t * 128, 64), 128), lanes)[1]
                g_ref[:, to] = g_ref[:, to] + dot(joined(both, slice(R0, T0), lanes)[0], right)
            update(x_ref, t)

        if b:
            pl.loop(0, b)(functools.partial(body, earlier=True))
        if b == 0:
            pl.loop(0, 4)(functools.partial(body, earlier=False))
        service(b, 1)
        pl.loop(b or 4, 8)(functools.partial(body, earlier=False))
        service(b, 2)
        now[T0:I0, :] = now[T0:I0, :] + mask_p_ref[:, block(b)]
        inv_h, inv_l = split2(x_ref[:, 128:])
        wh, wl = split2(now[rows, :])
        out = dot(jnp.concatenate([wh, wh, wl], axis=1), jnp.concatenate([inv_h, inv_l, inv_h], axis=1))
        h, l = split2(out)
        hi_ref[rows, block(b)] = h
        lo_ref[rows, block(b)] = l
        whit_ref[:, block(b)] = out[T0 - low : I0 - low]
        if b < 7:
            later[rows, :] = later[rows, :] - dot(jnp.concatenate([h, h, l], axis=1), jnp.concatenate([h, l, h], axis=1)[:128])

    left = joined(both, slice(R0, T0), block(7))[0]
    g_ref[...] = g_ref[...] + dot(left, joined(both, slice(I0, I0 + n), block(7))[1])

    @pl.loop(0, 4)
    def _(g):
        gh, gl = split2(g_ref[...])
        taken = jnp.dot(gh, s_ref[g, :n, :], preferred_element_type=f32) + jnp.dot(gl, s_ref[g, :n, :], preferred_element_type=f32)
        h_ref[g] = (s_ref[g, R0:C0, :].astype(f32) - taken).astype(bf16)

    service(8, 0)
    same = jnp.where(cols_at == panel * n, ridge, 0.0)

    @pl.loop(0, 4)
    def _(j):
        at = pl.multiple_of(j * 256, 256)
        acc = dot(h_ref[0], s_ref[0, pl.ds(C0 + at, 256), :])
        for g in range(1, 4):
            acc = acc + dot(h_ref[g], s_ref[g, pl.ds(C0 + at, 256), :])
        ids = iota((nr, 256), 0) + (rows_at - cols_at - at)
        acc = acc * (1.0 / samples) + jnp.where(ids == iota((nr, 256), 1), ridge, 0.0)
        cond_ref[:, pl.ds(at, 256)] = acc - same * g_ref[:, pl.ds(at, 256)]

    th, tl = hi_ref[T0:I0, :], lo_ref[T0:I0, :]
    rh, rl = hi_ref[R0:T0, :], lo_ref[R0:T0, :]
    res_ref[...] = mask_r_ref[...] - (dot(th, rh) + dot(th, rl) + dot(tl, rh))


def eliminate_scratch():
    return [
        pltpu.VMEM((128, 256), f32),
        pltpu.VMEM((2, I0 + n, 128), f32),
        pltpu.VMEM((I0 + n, n), bf16),
        pltpu.VMEM((I0 + n, n), bf16),
        pltpu.VMEM((nr, n), f32),
        pltpu.VMEM((4, nr, samples // 4), bf16),
    ]


def gather(ins, panel_ref, g_ref, f_ref, tr_ref, tm_ref, s_ref, mp_ref, mk_ref, own_ref, yb, pp, xb, ym, pm, xm, yc, sems, meanwhile, early):
    (ins_sem, y1s, y1r, x1s, x1r, z1s, z1r, d1s, d1r, z0s, z0r, d0s, d0r, y2s, y2r, x2s, x2r, x3s, yms, ymr, xms, xmr, dms, dmr) = sems
    s = lax.axis_index("samp")
    r = lax.axis_index("row")
    c = lax.axis_index("col")
    y, x = r // 4, lax.rem(r, 4)
    zh, core = c // 2, lax.rem(c, 2)
    q = lax.rem(panel_ref[0], 8)

    def at(dy=0, dx=0, dz=0, core_to=None):
        ny = lax.rem(y + dy + 4, 4)
        nx = lax.rem(x + dx + 4, 4)
        nz = lax.rem(zh * 4 + s + dz + 16, 16)
        k = core if core_to is None else core_to
        return (lax.rem(nz, 4), ny * 4 + nx, nz // 4 * 2 + k)

    loads = [pltpu.make_async_copy(src, dst, ins_sem.at[i]) for i, (src, dst) in enumerate(zip(ins, (g_ref, f_ref, tr_ref, tm_ref)))]
    for load in loads:
        load.start()
    sibling = at(core_to=1 - core)
    sent, across = [], []

    def remote(src, dst, send, recv, to, kept=sent):
        copy = pltpu.make_async_remote_copy(src_ref=src, dst_ref=dst, send_sem=send, recv_sem=recv, device_id=to, device_id_type=MESH)
        copy.start()
        kept.append(copy)

    def landed(ref, sem):
        pltpu.make_async_copy(ref, ref, sem).wait()

    barrier = pltpu.get_barrier_semaphore()
    partners = [at(dy=d) for d in (-1, 1)]
    partners += [at(dx=d, core_to=k) for d in (-1, 1) for k in (0, 1)]
    partners += [at(dz=d) for d in (-1, 1)] + [sibling]
    for to in partners:
        pl.semaphore_signal(barrier, inc=1, device_id=to, device_id_type=MESH)
    for load in loads:
        load.wait()
    freq = f_ref[...]
    spread = jnp.sqrt(2.0 * freq * (1.0 - freq))

    def standardize(k):
        lanes = slice(k * 128, (k + 1) * 128)
        value = (g_ref[:, lanes].astype(f32) - 2.0 * freq[:, lanes]) / spread[:, lanes]
        own_ref[lanes, :] = value.T.astype(bf16)

    standardize(0)
    pl.semaphore_wait(barrier, len(partners))

    half = pl.multiple_of(core * 256, 256)
    mrow = pl.multiple_of(core * 32, 32)
    def send(src, slots, ss, rs, ways):
        for i in range(2):
            remote(src, slots.at[i], ss.at[i], rs.at[i], ways[i])

    def pass_on(slots, size, ss, rs, ways):
        for i in range(2):
            landed(slots.at[i], rs.at[i])
            part = pl.ds(i * size, size)
            remote(slots.at[i, part], slots.at[2, part], ss.at[2 + i], rs.at[2 + i], ways[i])

    def opposite(slots, size, rs):
        for i in range(2):
            landed(slots.at[2, pl.ds(i * size, size)], rs.at[2 + i])

    def pick(distance, mine, slots):
        out = jnp.where(distance == 1, slots[1], mine)
        out = jnp.where(distance == 3, slots[0], out)
        return jnp.where(distance == 2, slots[2], out)

    along_y, along_x = (at(dy=1), at(dy=-1)), (at(dx=1), at(dx=-1))
    along_z = (at(dz=1), at(dz=-1))
    def send_y(k):
        send(own_ref.at[pl.ds(pl.multiple_of(k * 128 + core * 64, 64), 64)], yb[k], y1s.at[k], y1r.at[k], along_y)

    send_y(0)
    standardize(1)
    send_y(1)
    standardize(2)
    standardize(3)

    def send_z(src, base, size, ss, rs):
        for i in range(2):
            remote(src, s_ref.at[s, pl.ds(base, size)], ss.at[i], rs.at[i], along_z[i])

    def pass_on_z(base, size, ss, rs):
        for i in range(2):
            group = lax.rem(s + (3 if i == 0 else 1), 4)
            landed(s_ref.at[group, pl.ds(base, size)], rs.at[i])
            part = s_ref.at[group, pl.ds(pl.multiple_of(base + i * size // 2, 32), size // 2)]
            remote(part, part, ss.at[2 + i], rs.at[2 + i], along_z[i])

    def opposite_z(base, size, rs):
        for i in range(2):
            landed(s_ref.at[lax.rem(s + 2, 4), pl.ds(pl.multiple_of(base + i * size // 2, 32), size // 2)], rs.at[2 + i])

    row_base = pl.multiple_of(n + half, 256)
    send_z(own_ref.at[pl.ds(half, 256)], row_base, 256, z0s, z0r)
    s_ref[s, pl.ds(row_base, 256), :] = own_ref[pl.ds(half, 256), :]
    mk_ref[...] = tr_ref[...] * tm_ref[...].astype(f32)
    dy = lax.rem(q // 2 - y + 4, 4)

    def panel_base(k, h):
        return pl.multiple_of(h * 512 + k * 128 + core * 64, 64)

    def turn_x(k):
        opposite(yb[k], 32, y1r.at[k])
        mine = own_ref[pl.ds(pl.multiple_of(k * 128 + core * 64, 64), 64), :]
        pp[k, :, :] = pick(dy, mine, [yb[k][i] for i in range(3)])
        send(pp.at[k], xb[k], x1s.at[k], x1r.at[k], along_x)

    def turn_z(k):
        opposite(xb[k], 32, x1r.at[k])
        for h in range(2):
            dx = lax.rem(lax.rem(q, 2) * 2 + h - x + 4, 4)
            base = panel_base(k, h)
            s_ref[s, pl.ds(base, 64), :] = pick(dx, pp[k], [xb[k][i] for i in range(3)])
            send_z(s_ref.at[s, pl.ds(base, 64)], base, 64, z1s.at[k, h], z1r.at[k, h])

    def forward_z(k):
        for h in range(2):
            pass_on_z(panel_base(k, h), 64, z1s.at[k, h], z1r.at[k, h])

    def turn_core(k):
        for h in range(2):
            base = panel_base(k, h)
            opposite_z(base, 64, z1r.at[k, h])
            part = s_ref.at[:, pl.ds(base, 64)]
            remote(part, part, d1s.at[k, h], d1r.at[k, h], sibling, across)

    def forward_y(k):
        pass_on(yb[k], 32, y1s.at[k], y1r.at[k], along_y)
        if k < 2:
            send_y(k + 2)

    stages = (
        forward_y,
        turn_x,
        lambda k: pass_on(xb[k], 32, x1s.at[k], x1r.at[k], along_x),
        turn_z,
        forward_z,
        turn_core,
    )

    def wave(step):
        for behind in reversed(range(len(stages))):
            if 0 <= step - behind < 4:
                stages[behind](step - behind)

    wave(0)
    wave(1)
    send(mk_ref.at[pl.ds(mrow, 32)], ym, yms, ymr, along_y)
    meanwhile()
    pass_on_z(row_base, 256, z0s, z0r)
    wave(2)
    wave(3)
    pass_on(ym, 16, yms, ymr, along_y)
    wave(4)
    opposite_z(row_base, 256, z0r)
    mine = s_ref.at[:, pl.ds(row_base, 256)]
    remote(mine, mine, d0s.at[0], d0r.at[0], sibling, across)

    dist = lax.rem(y - zh + 4, 4)
    target = x // 2
    slot = lax.rem(x, 2) * 2 + core

    def half_of(i):
        return yc.at[pl.ds(2 * i, 2)]

    def to_y(i, src, sem, dy):
        pltpu.make_async_remote_copy(src_ref=src, dst_ref=half_of(i), send_sem=sem, recv_sem=y2r.at[i], device_id=at(dy=dy),
                                     device_id_type=MESH).start()

    @pl.when(dist == 0)
    def _():
        parts = [s_ref.at[2 * i : 2 * i + 2, pl.ds(row_base, 256)] for i in range(2)]
        for i, dy in ((0, 1), (1, -1), (1, 1), (0, -1)):
            to_y(i, parts[i], y2s.at[i, (dy + 1) // 2], dy)
        for i in range(2):
            pltpu.make_async_copy(parts[i], half_of(i), y2r.at[i]).start()

    opposite(ym, 16, ymr)
    pm[...] = pick(dy, mk_ref[pl.ds(mrow, 32), :], [ym[i] for i in range(3)])
    send(pm, xm, xms, xmr, along_x)

    def place(i, which):
        return s_ref.at[pl.ds(2 * i, 2), pl.ds(pl.multiple_of(n + nr + which * 256, 256), 256)]

    def to_x(i, src, which, sem, dx, k):
        pltpu.make_async_remote_copy(src_ref=src, dst_ref=place(i, which), send_sem=sem, recv_sem=x2r.at[which, i],
                                     device_id=at(dx=dx, core_to=k), device_id_type=MESH).start()

    def order(step):
        return jnp.where(dist == 3, 1 - step, step)

    def spread_half(step):
        i = order(step)
        landed(half_of(i), y2r.at[i])
        if step == 0:

            @pl.when(dist == 1)
            def _():
                to_y(0, half_of(0), y2s.at[0, 1], 1)

            @pl.when(dist == 3)
            def _():
                to_y(1, half_of(1), y2s.at[1, 0], -1)

        for dx in (1, -1):
            to_x(i, half_of(i), slot, x2s.at[i, (dx + 1) // 2], dx, target)

        @pl.when(core == target)
        def _():
            pltpu.make_async_copy(half_of(i), place(i, slot), x2r.at[slot, i]).start()

        @pl.when(core != target)
        def _():
            to_x(i, half_of(i), slot, x2s.at[i, 2], 0, 1 - core)

    def spread_near(step):
        @pl.when(dist != 2)
        def _():
            spread_half(step)

    def spread_far(step):
        @pl.when(dist == 2)
        def _():
            spread_half(step)

    def relayed(i, e):
        return lax.rem(x - (core * 2 + e) + 4, 4) == 1 + 2 * i

    def relay(step):
        i = order(step)
        for e in range(2):

            @pl.when(relayed(i, e))
            def _():
                for c2 in range(2):
                    which = e * 2 + c2
                    landed(place(i, which), x2r.at[which, i])
                    to_x(i, place(i, which), which, x3s.at[which, i], 1 - 2 * i, core)

    def arrive():
        for i in range(2):
            for e in range(2):

                @pl.when(jnp.logical_not(relayed(i, e)))
                def _():
                    for c2 in range(2):
                        landed(place(i, e * 2 + c2), x2r.at[e * 2 + c2, i])

    wave(5)
    def come(k):
        for h in range(2):
            across[1 + 2 * k + h].wait_recv()
            early(h * 512 + k * 128, 128)

    wave(6)
    pass_on(xm, 16, xms, xmr, along_x)
    across[0].wait_recv()
    come(0)
    early(n, nr)
    wave(7)
    spread_near(0)
    come(1)
    wave(8)
    come(2)
    come(3)

    def scores(step):
        part = mp_ref.at[pl.ds(mrow, 32)]
        if step == 0:
            opposite(xm, 16, xmr)
            for h in range(2):
                dx = lax.rem(lax.rem(q, 2) * 2 + h - x + 4, 4)
                mp_ref[pl.ds(mrow, 32), h * 512 : (h + 1) * 512] = pick(dx, pm[...], [xm[i] for i in range(3)])
            remote(part, part, dms.at[0], dmr.at[0], sibling)
        else:
            landed(part, dmr.at[0])

    def drain():
        for copy in sent + across:
            copy.wait_send()
        for i in range(2):

            @pl.when(dist == 0)
            def _():
                for j in range(2):
                    landed(half_of(i), y2s.at[i, j])

            @pl.when(dist == 1 + 2 * i)
            def _():
                landed(half_of(i), y2s.at[i, 1 - i])

            for j in range(2):
                landed(half_of(i), x2s.at[i, j])

            @pl.when(core != target)
            def _():
                landed(half_of(i), x2s.at[i, 2])

            for e in range(2):

                @pl.when(relayed(i, e))
                def _():
                    for c2 in range(2):
                        landed(place(i, e * 2 + c2), x3s.at[e * 2 + c2, i])

    return spread_near, spread_far, relay, arrive, scores, drain


def on_device(genotypes, frequencies, trait_scores, typed_mask, panel_index):
    dma = pltpu.SemaphoreType.DMA
    hbm, vmem = pl.BlockSpec(memory_space=pltpu.HBM), pl.BlockSpec(memory_space=pltpu.VMEM)
    own = eliminate_scratch()
    gathered = [
        pltpu.VMEM((512, 512), jnp.int32),
        pltpu.VMEM((1, 512), f32),
        pltpu.VMEM((traits, 512), f32),
        pltpu.VMEM((1, 512), jnp.int32),
        pltpu.VMEM((4, C0 + nc, 512), bf16),
        pltpu.VMEM((traits, n), f32),
        pltpu.VMEM((traits, 512), f32),
        pltpu.VMEM((512, 512), bf16),
        *[pltpu.VMEM((3, 64, 512), bf16)] * 4,
        pltpu.VMEM((4, 64, 512), bf16),
        *[pltpu.VMEM((3, 64, 512), bf16)] * 4,
        pltpu.VMEM((3, 32, 512), f32),
        pltpu.VMEM((32, 512), f32),
        pltpu.VMEM((3, 32, 512), f32),
        pltpu.VMEM((4, 256, 512), bf16),
    ]
    sems = [dma(shape) for shape in (
        (4,), (4, 4), (4, 4), (4, 4), (4, 4), (4, 2, 4), (4, 2, 4), (4, 2), (4, 2), (4,), (4,), (1,), (1,),
        (2, 2), (2,), (2, 3), (4, 2), (4, 2), (4,), (4,), (4,), (4,), (1,), (1,))]

    def kernel(g, f, tr, tm, panel_ref, cond_ref, whit_ref, res_ref, *rest):
        work, rest = rest[: len(own)], rest[len(own) :]
        bufs, rest = rest[: len(gathered)], rest[len(gathered) :]
        s_ref, mp_ref, mk_ref = bufs[4], bufs[5], bufs[6]
        yb, xb = bufs[8:12], bufs[13:17]

        def meanwhile():
            for ref in work[2:4]:
                ref[I0:, :] = jnp.zeros((n, n), bf16)
            work[4][...] = jnp.zeros((nr, n), f32)

        def early(first, count):
            part = slice(first, first + count)
            acc = dot(s_ref[0, part, :], s_ref[0, :128, :])
            for g in range(1, 4):
                acc = acc + dot(s_ref[g, part, :], s_ref[g, :128, :])
            work[1][0, part, :] = acc * (1.0 / samples)

        spread_near, spread_far, relay, arrive, scores, drain = gather(
            (g, f, tr, tm), panel_ref, *bufs[:8], yb, bufs[12], xb, *bufs[17:], rest, meanwhile, early)
        steps = {(0, 1): (lambda: scores(0),), (0, 2): (lambda: scores(1),),
                 (1, 0): (lambda: spread_near(1), lambda: spread_far(0)), (2, 0): (lambda: spread_far(1),),
                 (4, 0): (lambda: relay(0),), (6, 0): (lambda: relay(1),), (8, 0): (arrive,)}

        def service(b, part):
            for step in steps.get((b, part), ()):
                step()

        eliminate(lax.rem(panel_ref[0], 8), lax.axis_index("row") * 512, lax.axis_index("col") * 1024,
                  s_ref, mp_ref, mk_ref, cond_ref, whit_ref, res_ref, *work, service=service)
        drain()

    return pl.pallas_call(
        kernel,
        out_shape=(
            jax.ShapeDtypeStruct((nr, nc), f32),
            jax.ShapeDtypeStruct((traits, n), f32),
            jax.ShapeDtypeStruct((traits, nr), f32),
        ),
        in_specs=[hbm] * 4 + [pl.BlockSpec(memory_space=pltpu.SMEM)],
        out_specs=(vmem,) * 3,
        scratch_shapes=own + gathered + sems,
        compiler_params=pltpu.CompilerParams(vmem_limit_bytes=44 * 1024 * 1024, collective_id=0, has_side_effects=True),
    )(*(pltpu.with_memory_space_constraint(a, pltpu.HBM) for a in (genotypes, frequencies[None, :], trait_scores, typed_mask[None, :])), panel_index)


def solution(mesh):
    placed = (P("samp", "row"), P("row"), P(None, "row"), P("row"), P())
    return jax.shard_map(
        on_device,
        mesh=mesh,
        in_specs=placed,
        out_specs=(P("row", "col"), P(), P(None, "row")),
        check_vma=False,
    )
```
